32 devices in a mesh: tm: 16 (over z, y, x), elem: 2 (over core).
Axes of the slice: x: 2, y: 2, z: 4, core: 2. Of those that a mesh axis runs over, the one named last changes fastest.
Arguments:
- history: float32 [128, 16384], P('tm', 'elem'), may hold values from -6 to 6
- points: float32 [3, 16384], P(None, 'elem'), may hold values from -3 to 3
- areas: float32 [16384], P('elem'), may hold values from 0.3 to 3
- ownership: int32 [16384], P('elem'), may hold values from 0 to 8191, as said below
- block_rows: int32 [384], replicated, may hold values from 0 to 63, as said below
- block_cols: int32 [384], replicated, may hold values from 0 to 127, as said below
- block_live: int32 [2], replicated, may hold values from 64 to 192, as said below
Outputs:
- response: float32 [128, 16384], P('tm', 'elem')
The draws below stay inside these ranges and needn't reach their ends.
Inputs may be any that keep to these rules, and one draw needn't show every extreme that they name: `ownership`: each aligned block of 8192 entries belonging to one group is a permutation of 0 to 8191. `block_rows`: slot k < 64 of every group holds k; slots at and after a group's block_live are unused. `block_cols`: slot k < 64 of group g holds g * 64 + k; slot 64 + j of group g holds a cluster of group (g + 1 + j) mod 2. `block_live`: one group has exactly 192 live slots, every other group at most 128, so the counts sum to at most 320.
All inputs are finite; a program needn't handle non-finite values.
Results may differ from the reference program's by a relative error of at most 0.0003.
Values sent between devices are 32-bit elements; how exact they have to be, the bound alone decides.
No kernel may reach another device: no remote copies, remote signals or barrier semaphores. Data moves between devices by JAX's collectives and lax.ppermute only.
A program may use at most 128 MiB of HBM per device.

```python
import math
import jax
import jax.numpy as jnp
from jax import lax

FS = 4
E_DEV = 8192
CLUSTER = 128
STEPS = 128
ELEMENTS = 16384
CL_DEV = 64
CLUSTERS = 128
BCAP = 192
SHARE = 160
N_TM = 16
N_ELEM = 2


def pattern_parts(key):
    group_count = CLUSTERS // CL_DEV
    group_ids = jnp.arange(group_count, dtype=jnp.int32)
    busiest = jax.random.randint(jax.random.fold_in(key, 11), (), 0, group_count, dtype=jnp.int32)
    others = jax.random.randint(jax.random.fold_in(key, 12), (group_count,), CL_DEV, 2 * CL_DEV + 1, dtype=jnp.int32)
    live_count = jnp.where(group_ids == busiest, BCAP, others).astype(jnp.int32)
    slot_ids = jnp.arange(BCAP, dtype=jnp.int32)[None, :]
    random_rows = jax.random.randint(jax.random.fold_in(key, 13), (group_count, BCAP), 0, CL_DEV, dtype=jnp.int32)
    row_table = jnp.where(slot_ids < CL_DEV, slot_ids, random_rows)
    random_inner = jax.random.randint(jax.random.fold_in(key, 14), (group_count, BCAP), 0, CL_DEV, dtype=jnp.int32)
    peer_group = (group_ids[:, None] + 1 + (slot_ids - CL_DEV)) % group_count
    col_table = jnp.where(slot_ids < CL_DEV, group_ids[:, None] * CL_DEV + slot_ids, peer_group * CL_DEV + random_inner)
    return (row_table.reshape(-1).astype(jnp.int32), col_table.reshape(-1).astype(jnp.int32), live_count)


def draw_block_rows(key, part):
    return pattern_parts(key)[0]


def draw_block_cols(key, part):
    return pattern_parts(key)[1]


def draw_block_live(key, part):
    return pattern_parts(key)[2]


def one_permutation(sub_key):
    return jax.random.permutation(sub_key, E_DEV)


def draw_ownership(key, part):
    group_count = ELEMENTS // E_DEV
    perm_keys = jax.random.split(jax.random.fold_in(key, 21), group_count)
    return jax.vmap(one_permutation)(perm_keys).reshape(-1).astype(jnp.int32)


def shard_levels(rng, dims, cuts, least, largest):
    gain, own = 1.0, jax.random.fold_in(rng, 6)
    for dim, parts in cuts:
        heights = jnp.exp(jax.random.uniform(jax.random.fold_in(own, dim), (parts,), jnp.float32, least / len(cuts), largest / len(cuts)))
        gain = gain * jnp.repeat(heights, dims[dim] // parts).reshape([-1 if axis == dim else 1 for axis in range(len(dims))])
    return gain


def centred(stream_key, extent, deviation, most, pieces=(), held_as=jnp.bfloat16):
    drawn = jax.random.normal(stream_key, extent, jnp.float32) * deviation
    if len(pieces) > 0:
        drawn = shard_levels(stream_key, extent, pieces, -0.22, 0.18) * drawn
    return jnp.clip(drawn, min=-most, max=most).astype(held_as)


def setup_inputs(seed: int = 0) -> dict:
    keys = jax.random.split(jax.random.key(seed), 8)
    history = centred(keys[0], (STEPS, ELEMENTS), 1.0, 6.0, ((0, 16), (1, 2)), jnp.float32)
    points = centred(keys[1], (3, ELEMENTS), 0.5, 3.0, ((1, 2),), jnp.float32)
    areas = jnp.clip(jnp.exp(math.log(3.0) - 2.3025851 * jax.random.uniform(keys[2], (ELEMENTS,), jnp.float32) ** shard_levels(keys[2], (ELEMENTS,), ((0, 2),), -0.2, 0.2)), 0.3, 3.0)
    ownership = draw_ownership(jax.random.fold_in(keys[7], 71), 0)
    block_rows = draw_block_rows(jax.random.fold_in(keys[7], 71), 0)
    block_cols = draw_block_cols(jax.random.fold_in(keys[7], 71), 0)
    block_live = draw_block_live(jax.random.fold_in(keys[7], 71), 0)
    return dict(history=history, points=points, areas=areas, ownership=ownership, block_rows=block_rows, block_cols=block_cols, block_live=block_live)


LOG_HALF = 0.6931471805599453
SOFTEN = 0.05
INV_STEP = 4.0
FOUR_PI = 4.0 * math.pi

def transform_tables(steps_total, freqs):
    time_ids = jnp.arange(steps_total, dtype=jnp.int32)
    levels = jnp.arange(freqs, dtype=jnp.int32)
    scale_angle = 2.0 * math.pi / steps_total
    phase_fwd = (levels[:, None] * time_ids[None, :] % steps_total).astype(jnp.float32) * scale_angle
    decay_rate = jnp.exp(time_ids.astype(jnp.float32) * (-LOG_HALF / steps_total))
    forward = jnp.concatenate([jnp.cos(phase_fwd) * decay_rate[None, :], -jnp.sin(phase_fwd) * decay_rate[None, :]], axis=0)
    phase_inv = (time_ids[:, None] * levels[None, :] % steps_total).astype(jnp.float32) * scale_angle
    growth = jnp.exp(time_ids.astype(jnp.float32) * (LOG_HALF / steps_total)) / steps_total
    weight = jnp.where(levels == 0, 1.0, 2.0).astype(jnp.float32)
    factor = growth[:, None] * weight[None, :]
    inverse = jnp.concatenate([jnp.cos(phase_inv) * factor, -jnp.sin(phase_inv) * factor], axis=1)
    return (forward, inverse)

def laplace_values(first_freq, freq_count, steps_total):
    freq_index = (first_freq + jnp.arange(freq_count, dtype=jnp.int32)).astype(jnp.float32)
    angles = freq_index * (2.0 * math.pi / steps_total)
    radius = math.exp(-LOG_HALF / steps_total)
    real_part = 1.0 - radius * jnp.cos(angles)
    imag_part = -radius * jnp.sin(angles)
    delta_re = real_part + 0.5 * (real_part * real_part - imag_part * imag_part)
    delta_im = imag_part + real_part * imag_part
    return (INV_STEP * delta_re, INV_STEP * delta_im)

def block_terms(row_points, col_points, col_area, col_values, lap_real, lap_imag):
    separation = row_points[:, :, :, None] - col_points[:, :, None, :]
    distance = jnp.sqrt(lax.optimization_barrier(jnp.sum(separation * separation, axis=0)) + SOFTEN * SOFTEN)
    base_kernel = col_area[:, None, :] / (FOUR_PI * distance)
    rows_real = []
    rows_imag = []
    for freq_pos in range(lap_real.shape[0]):
        damping = base_kernel * jnp.exp(-lap_real[freq_pos] * distance)
        phase_arg = lap_imag[freq_pos] * distance
        kernel_re = damping * jnp.cos(phase_arg)
        kernel_im = -damping * jnp.sin(phase_arg)
        source_re = col_values[0, freq_pos][:, None, :]
        source_im = col_values[1, freq_pos][:, None, :]
        rows_real.append(lax.optimization_barrier(jnp.sum(kernel_re * source_re - kernel_im * source_im, axis=-1)))
        rows_imag.append(lax.optimization_barrier(jnp.sum(kernel_re * source_im + kernel_im * source_re, axis=-1)))
    return jnp.stack([jnp.stack(rows_real), jnp.stack(rows_imag)])

def reference(history, points, areas, ownership, block_rows, block_cols, block_live):
    steps_total, elements = history.shape
    freqs = FS * N_TM
    group_count = N_ELEM
    forward, inverse = transform_tables(steps_total, freqs)
    spectra = jnp.dot(forward, history, precision=lax.Precision.HIGHEST)
    global_order = (ownership + jnp.arange(elements, dtype=jnp.int32) // E_DEV * E_DEV).astype(jnp.int32)
    clusters_total = elements // CLUSTER
    cluster_values = spectra.reshape(2, freqs, elements)[:, :, global_order].reshape(2, freqs, clusters_total, CLUSTER)
    cluster_coords = points[:, global_order].reshape(3, clusters_total, CLUSTER)
    cluster_area = areas[global_order].reshape(clusters_total, CLUSTER)
    lap_real, lap_imag = laplace_values(0, freqs, steps_total)
    live_ends = jnp.cumsum(block_live).astype(jnp.int32)
    live_starts = (live_ends - block_live).astype(jnp.int32)
    capacity = group_count * SHARE
    slot_width = math.gcd(16, capacity)
    freq_band = math.gcd(16, freqs)
    slot_ids = jnp.arange(capacity, dtype=jnp.int32)
    owner_group = jnp.minimum(lax.optimization_barrier(jnp.sum((slot_ids[:, None] >= live_ends[None, :]).astype(jnp.int32), axis=1)).astype(jnp.int32), group_count - 1)
    offset = slot_ids - live_starts[owner_group]
    slot_live = slot_ids < live_ends[group_count - 1]
    flat_index = (owner_group * BCAP + jnp.clip(offset, 0, BCAP - 1)).astype(jnp.int32)
    rows_global = (owner_group * CL_DEV + block_rows[flat_index]).astype(jnp.int32)
    col_ids = block_cols[flat_index]
    band_starts = jnp.arange(freqs // freq_band, dtype=jnp.int32) * freq_band

    def slot_step(target, inputs):
        row_ids, col_now, live_now = inputs
        row_points = cluster_coords[:, row_ids]
        col_points = cluster_coords[:, col_now]
        col_area = cluster_area[col_now]
        slot_mask = live_now.astype(jnp.float32)[None, None, :, None]

        def band_step(running, band_start):
            levels = (band_start + jnp.arange(freq_band, dtype=jnp.int32)).astype(jnp.int32)
            col_values = cluster_values[:, levels[:, None], col_now[None, :]]
            block_out = block_terms(row_points, col_points, col_area, col_values, lap_real[levels], lap_imag[levels]) * slot_mask
            return (running.at[:, levels[:, None], row_ids[None, :]].add(block_out), None)
        target, _ = lax.scan(band_step, target, band_starts)
        return (target, None)
    near_field = jnp.zeros((2, freqs, clusters_total, CLUSTER), jnp.float32)
    near_field, _ = lax.scan(slot_step, near_field, (rows_global.reshape(-1, slot_width), col_ids.reshape(-1, slot_width), slot_live.reshape(-1, slot_width)))
    element_near = jnp.zeros((2, freqs, elements), jnp.float32).at[:, :, global_order].set(near_field.reshape(2, freqs, elements))
    return jnp.dot(inverse, element_near.reshape(2 * freqs, elements), precision=lax.Precision.HIGHEST)
```

```python
import functools
import math

import jax
import jax.numpy as jnp
import numpy as np
from jax import lax
from jax.experimental import pallas as pl
from jax.experimental.pallas import tpu as pltpu
from jax.sharding import PartitionSpec as P

FS = 4
CLUSTER = 128
LANES = 128
LOG_HALF = 0.6931471805599453
SOFTEN = 0.05
INV_STEP = 4.0
FOUR_PI = 4.0 * math.pi
LOW = 256
F32 = jnp.float32
BF16 = jnp.bfloat16


def fit(func, high, degree):
    nodes = (np.cos((np.arange(600) + 0.5) / 600 * np.pi) + 1) * (high / 2)
    series = np.polynomial.chebyshev.Chebyshev.fit(
        nodes, func(nodes), degree, domain=[0, high]
    )
    return [float(v) for v in series.convert(kind=np.polynomial.Polynomial).coef]


SIN_HALF = fit(lambda u: math.sqrt(2) * np.sin(np.pi * np.sqrt(u)) / np.sqrt(u), 0.25, 3)
COS_HALF = fit(lambda u: math.sqrt(2) * np.cos(np.pi * np.sqrt(u)), 0.25, 4)
ARCTAN = fit(lambda u: np.arctan(np.sqrt(u)) / np.sqrt(u) / (2 * np.pi), 1.0, 9)


def poly(coefs, u):
    total = jnp.full_like(u, coefs[-1])
    for value in coefs[-2::-1]:
        total = total * u + value
    return total


def transform_tables(steps, freqs):
    time_ids = np.arange(steps)
    levels = np.arange(freqs)
    phase = (levels[:, None] * time_ids[None, :] % steps) * (2.0 * np.pi / steps)
    decay = np.exp2(-time_ids / steps)
    forward = np.stack([np.cos(phase) * decay, -np.sin(phase) * decay])
    weight = np.where(levels == 0, 1.0, 2.0)[:, None] / (decay * steps)[None, :]
    inverse = np.stack([np.cos(phase) * weight, -np.sin(phase) * weight])
    return forward, inverse


def laplace_table(freqs, steps):
    angles = np.arange(freqs) * (2.0 * np.pi / steps)
    zeta = math.exp(-LOG_HALF / steps) * np.exp(1j * angles)
    delta = (1.0 - zeta) + 0.5 * (1.0 - zeta) ** 2
    return INV_STEP * delta


def packed_tables(steps, freqs, split):
    forward, inverse = transform_tables(steps, freqs)
    each = FS // split
    dests = freqs // each
    fwd = np.zeros((dests, 2, split, each, split, steps), np.float64)
    inv = np.zeros((dests, 2, split, each, split, steps), np.float64)
    for half in range(split):
        rows = forward.reshape(2, dests, each, steps).transpose(1, 0, 2, 3)
        fwd[:, :, half, :, half, :] = rows
        rows = inverse.reshape(2, dests, each, steps).transpose(1, 0, 2, 3)
        inv[:, :, half, :, half, :] = rows
    fwd = fwd.reshape(dests * 2 * FS, split * steps)
    inv = inv.reshape(dests * 2 * FS, split * steps).T
    return fwd.astype(np.float32), np.ascontiguousarray(inv).astype(np.float32)


def parts_of(x, count):
    out = []
    for _ in range(count - 1):
        head = x.astype(BF16).astype(F32)
        out.append(head)
        x = x - head
    return out + [x]


def one_hot_low(low_row):
    width = low_row.shape[1]
    ids = lax.broadcasted_iota(jnp.int32, (LOW, width), 0)
    return jnp.where(ids == low_row, 1.0, 0.0).astype(BF16)


def gather_body(own_ref, lhs_ref, high_count, chunk, emit):
    def step(c, _):
        at = pl.multiple_of(c * chunk, chunk)
        own = own_ref[:, pl.ds(at, chunk)]
        high = jnp.broadcast_to(own >> 8, (8, chunk))
        hot = one_hot_low(own & (LOW - 1))
        picked = jnp.dot(lhs_ref[...], hot, preferred_element_type=F32)
        top = jnp.zeros((8, chunk), F32)
        bottom = jnp.zeros((8, chunk), F32)
        for h in range(high_count):
            mask = high == h
            top += jnp.where(mask, picked[16 * h : 16 * h + 8], 0.0)
            bottom += jnp.where(mask, picked[16 * h + 8 : 16 * h + 16], 0.0)
        emit(c, top, bottom)
        return 0

    lax.fori_loop(0, own_ref.shape[1] // chunk, step, 0)


def order_history_kernel(own_ref, hist_ref, out_ref, lhs_ref):
    elems = own_ref.shape[1]
    width = out_ref.shape[2]
    chunk = min(256, width)
    for h in range(elems // LOW):
        pieces = parts_of(hist_ref[:, LOW * h : LOW * h + LOW], 2)
        lhs_ref[16 * h : 16 * h + 16, :] = jnp.concatenate(pieces, axis=0).astype(BF16)
    per = width // chunk

    def emit(c, top, bottom):
        at = pl.multiple_of(lax.rem(c, per) * chunk, chunk)
        out_ref[c // per, :, pl.ds(at, chunk)] = top + bottom

    gather_body(own_ref, lhs_ref, elems // LOW, chunk, emit)


def order_history(own, history, width):
    steps, elems = history.shape
    return pl.pallas_call(
        order_history_kernel,
        out_shape=jax.ShapeDtypeStruct((elems // width, steps, width), F32),
        scratch_shapes=[pltpu.VMEM((elems // LOW * 16, LOW), BF16)],
        name="order_history",
    )(own, history)


def order_geometry_kernel(own_ref, pts_ref, area_ref, out_ref, lhs_ref):
    elems = own_ref.shape[1]
    for h in range(elems // LOW):
        at = slice(LOW * h, LOW * h + LOW)
        rows = jnp.concatenate([pts_ref[:, at], area_ref[:, at] * (1.0 / FOUR_PI)], axis=0)
        pieces = parts_of(rows, 3) + [jnp.zeros_like(rows)]
        lhs_ref[16 * h : 16 * h + 16, :] = jnp.concatenate(pieces, axis=0).astype(BF16)

    def emit(c, top, bottom):
        total = top[0:4] + top[4:8] + bottom[0:4]
        total = jnp.concatenate([total, jnp.zeros_like(total)], axis=0)
        out_ref[2 * c] = total[:, :CLUSTER]
        out_ref[2 * c + 1] = total[:, CLUSTER:]

    gather_body(own_ref, lhs_ref, elems // LOW, 2 * CLUSTER, emit)


def order_geometry(own, points, areas):
    elems = own.shape[1]
    return pl.pallas_call(
        order_geometry_kernel,
        out_shape=jax.ShapeDtypeStruct((elems // CLUSTER, 8, CLUSTER), F32),
        scratch_shapes=[pltpu.VMEM((elems // LOW * 16, LOW), BF16)],
        name="order_geometry",
    )(own, points, areas)


def return_kernel(own_ref, near_ref, out_ref, lhs_ref, hot_ref, acc_ref):
    pieces_count, _, width = near_ref.shape
    elems = own_ref.shape[1]
    high_count = elems // LOW
    chunk = lhs_ref.shape[1]
    per = chunk // width
    acc_ref[...] = jnp.zeros_like(acc_ref)

    def step(c, _):
        at = pl.multiple_of(c * chunk, chunk)
        own = own_ref[:, pl.ds(at, chunk)]
        hot_ref[...] = one_hot_low(own & (LOW - 1))
        high = jnp.broadcast_to(own >> 8, (8, chunk))
        for p in range(per):
            lanes = slice(p * width, p * width + width)
            head, tail = parts_of(near_ref[c * per + p], 2)
            here = high[:, lanes]
            for h in range(high_count):
                mask = here == h
                both = [jnp.where(mask, head, 0.0), jnp.where(mask, tail, 0.0)]
                lhs_ref[16 * h : 16 * h + 16, lanes] = jnp.concatenate(both, axis=0).astype(BF16)
        acc_ref[...] += lax.dot_general(
            lhs_ref[...], hot_ref[...], (((1,), (1,)), ((), ())), preferred_element_type=F32
        )
        return 0

    lax.fori_loop(0, elems // chunk, step, 0)
    for h in range(high_count):
        out_ref[:, LOW * h : LOW * h + LOW] = (
            acc_ref[16 * h : 16 * h + 8, :] + acc_ref[16 * h + 8 : 16 * h + 16, :]
        )


def return_to_elements(own, values):
    pieces, steps, width = values.shape
    elems = own.shape[1]
    chunk = max(1024, width)
    return pl.pallas_call(
        return_kernel,
        out_shape=jax.ShapeDtypeStruct((steps, elems), F32),
        scratch_shapes=[
            pltpu.VMEM((elems // LOW * 16, chunk), BF16),
            pltpu.VMEM((LOW, chunk), BF16),
            pltpu.VMEM((elems // LOW * 16, LOW), F32),
        ],
        name="return_to_elements",
    )(own, values)


def forward_kernel(split, table_ref, x_ref, out_ref):
    steps, width = x_ref.shape
    half = width // split
    stacked = jnp.concatenate([x_ref[:, half * s : half * s + half] for s in range(split)], axis=0)
    out_ref[...] = jnp.dot(
        table_ref[...], stacked, precision=lax.Precision.HIGHEST, preferred_element_type=F32
    )


def forward_transform(table, x, split):
    return pl.pallas_call(
        functools.partial(forward_kernel, split),
        out_shape=jax.ShapeDtypeStruct((table.shape[0], x.shape[1] // split), F32),
        name="forward_transform",
    )(table, x)


def inverse_kernel(split, table_ref, x_ref, out_ref):
    total, half = x_ref.shape
    dests, steps_local, _ = out_ref.shape
    steps = dests * steps_local
    values = jnp.dot(
        table_ref[...], x_ref[...], precision=lax.Precision.HIGHEST, preferred_element_type=F32
    )
    for s in range(split):
        for d in range(dests):
            at = s * steps + d * steps_local
            out_ref[d, :, half * s : half * s + half] = values[at : at + steps_local]


def inverse_transform(table, x, split, dests):
    steps = table.shape[0] // split
    return pl.pallas_call(
        functools.partial(inverse_kernel, split),
        out_shape=jax.ShapeDtypeStruct((dests, steps // dests, x.shape[1] * split), F32),
        name="inverse_transform",
    )(table, x)


def near_kernel(
    cfg, meta, coef, rows, cols, live, geo_ref, val_ref, sel_ref, out_ref, acc_ref, col_ref, row_ref
):
    each, split, groups, group_clusters, cap, own_groups, per_piece, feats = cfg
    clusters = geo_ref.shape[0]
    per_half = per_piece // split
    pieces = group_clusters // per_piece
    width = 3 + 2 * each
    acc_ref[...] = jnp.zeros_like(acc_ref)

    const_rows = sel_ref[0 : 3 * feats, 0 : 3 * LANES]

    def prepare(piece, _):
        for g in range(groups):
            index = piece * groups + g if own_groups == groups else g * pieces + piece
            chunk = val_ref[index]
            re, im = chunk[0:FS], chunk[FS : 2 * FS]
            ax, ay = jnp.abs(re), jnp.abs(im)
            large, small = jnp.maximum(ax, ay), jnp.minimum(ax, ay)
            q = small / jnp.maximum(large, 1e-37)
            turn = q * poly(ARCTAN, q * q)
            turn = jnp.where(ay > ax, 0.25 - turn, turn)
            turn = jnp.where(re < 0, 0.5 - turn, turn)
            turn = jnp.where(im < 0, -turn, turn)
            size = large * jnp.sqrt(1.0 + q * q)
            for w in range(per_piece):
                c = g * group_clusters + piece * per_piece + w
                half, lane = w // per_half, (w % per_half) * LANES
                mine = slice(half * each, half * each + each)
                place = geo_ref[c]
                coords = place[0:3]
                found = [
                    coords,
                    turn[mine, lane : lane + LANES],
                    size[mine, lane : lane + LANES] * place[3:4],
                ]
                if feats > width:
                    found.append(jnp.zeros((feats - width, LANES), F32))
                feature = jnp.concatenate(found, axis=0)
                pieces3 = parts_of(feature, 3)
                ones = jnp.ones((feats, LANES), F32)
                stacked = jnp.concatenate(pieces3 + [ones], axis=0)
                col_ref[c] = stacked.T.astype(BF16)
                lines = []
                for part in range(3):
                    x3 = pieces3[part]
                    lines.append(jnp.concatenate([-x3[k : k + 1] for k in range(3)], axis=1))
                lines.append(jnp.zeros((feats - 3, 3 * LANES), F32))
                tail = jnp.concatenate(lines, axis=0)
                row_ref[c] = jnp.concatenate([const_rows, tail], axis=0).astype(BF16)
        return 0

    lax.fori_loop(0, pieces, prepare, 0)

    decay = [coef[f] for f in range(each)]
    turns = [coef[each + f] for f in range(each)]
    sel = sel_ref[:, 3 * LANES :].astype(BF16)

    for slot in range(own_groups):
        group = slot if own_groups == groups else meta[0]

        def block(b, _, group=group, slot=slot):
            at = group * cap + b
            row, col = rows[at], cols[at]
            left = col_ref[col]
            gaps = jnp.dot(left, row_ref[group * group_clusters + row], preferred_element_type=F32)
            spread = jnp.dot(left, sel, preferred_element_type=F32)
            sums = [jnp.zeros((8, LANES), F32) for _ in range(2 * each)]
            for j in range(CLUSTER // 8):
                js = slice(8 * j, 8 * j + 8)
                dx, dy, dz = (gaps[js, LANES * k : LANES * k + LANES] for k in range(3))
                square = dx * dx + dy * dy + dz * dz + SOFTEN * SOFTEN
                inv = lax.rsqrt(square)
                dist = square * inv
                for f in range(each):
                    psi = spread[js, LANES * f : LANES * f + LANES]
                    mag = spread[js, LANES * (each + f) : LANES * (each + f) + LANES]
                    weight = jnp.exp2(decay[f] * dist) * (inv * mag)
                    t = psi - turns[f] * dist
                    t = t - jnp.round(t)
                    u = t * t
                    s = t * poly(SIN_HALF, u)
                    c = poly(COS_HALF, u)
                    ws = weight * s
                    sums[f] += weight - ws * s
                    sums[each + f] += ws * c
            target = slot * group_clusters + row
            for i in range(2 * each):
                acc_ref[target, i] += sums[i]
            return 0

        lax.fori_loop(0, live[group], block, 0)

    def finish(piece, _):
        for slot in range(own_groups):
            for w in range(per_piece):
                c = slot * group_clusters + piece * per_piece + w
                half, lane = w // per_half, (w % per_half) * LANES
                total = jnp.sum(acc_ref[c], axis=1)
                dest = piece * own_groups + slot
                for part in range(2):
                    first = part * FS + half * each
                    out_ref[dest, first : first + each, lane : lane + LANES] = total[
                        part * each : part * each + each
                    ]
        return 0

    lax.fori_loop(0, pieces, finish, 0)


def near_field(meta, coef, rows, cols, live, geometry, values, split, groups, own_groups):
    each = FS // split
    clusters = geometry.shape[0]
    group_clusters = clusters // groups
    per_piece = values.shape[2] // LANES * split
    feats = -(-(3 + 2 * each) // 8) * 8
    width = 3 + 2 * each
    sel = np.zeros((4 * feats, width, LANES), np.float32)
    for part in range(3):
        for k in range(width):
            sel[part * feats + k, k] = 1.0
    sel = sel.reshape(4 * feats, width * LANES)
    cfg = (
        each,
        split,
        groups,
        group_clusters,
        rows.shape[0] // groups,
        own_groups,
        per_piece,
        feats,
    )
    smem = pl.BlockSpec(memory_space=pltpu.SMEM)
    vmem = pl.BlockSpec(memory_space=pltpu.VMEM)
    dests = own_groups * group_clusters // per_piece
    return pl.pallas_call(
        functools.partial(near_kernel, cfg),
        out_shape=jax.ShapeDtypeStruct((dests, 2 * FS, per_piece // split * LANES), F32),
        in_specs=[smem] * 5 + [vmem] * 3,
        out_specs=vmem,
        scratch_shapes=[
            pltpu.VMEM((own_groups * group_clusters, 2 * each, 8, LANES), F32),
            pltpu.VMEM((clusters, CLUSTER, 4 * feats), BF16),
            pltpu.VMEM((clusters, 4 * feats, 3 * LANES), BF16),
        ],
        compiler_params=pltpu.CompilerParams(vmem_limit_bytes=56 * 2**20),
        name="near_field",
    )(meta, coef, rows, cols, live, geometry, values, jnp.asarray(sel))


def per_device(history, points, areas, ownership, block_rows, block_cols, block_live):
    steps_local, elem_local = history.shape
    tm_count = lax.axis_size("tm")
    groups = lax.axis_size("elem")
    steps = steps_local * tm_count
    freqs = FS * tm_count
    width = elem_local // tm_count
    split = groups if groups == 2 and width % (2 * LANES) == 0 else 1
    each = FS // split
    shared = split == groups
    axes = ("tm", "elem") if shared else "tm"
    forward, inverse = packed_tables(steps, freqs, split)
    lap = laplace_table(freqs, steps).reshape(-1, each)
    coefs = np.concatenate([-lap.real / LOG_HALF, lap.imag / (2.0 * np.pi)], axis=1)
    my_group = lax.axis_index("elem")
    mine = lax.axis_index("tm") * split + (my_group if shared else 0)
    coef = lax.dynamic_index_in_dim(jnp.asarray(coefs.astype(np.float32)), mine, 0, keepdims=False)

    own = ownership.reshape(1, elem_local)
    pieces = order_history(own, history, width)
    by_time = lax.all_to_all(
        pieces.reshape(tm_count * steps_local, width), "tm", split_axis=0, concat_axis=0, tiled=True
    )
    geometry = order_geometry(own, points, areas.reshape(1, elem_local))
    geometry = lax.all_gather(geometry, "elem", axis=0, tiled=True)
    spectra = forward_transform(jnp.asarray(forward), by_time, split)
    slab = lax.all_to_all(spectra, axes, split_axis=0, concat_axis=0, tiled=True)
    if not shared:
        slab = lax.all_gather(slab, "elem", axis=0, tiled=True)
    slab = slab.reshape(-1, 2 * FS, width // split)
    near = near_field(
        jnp.full((1,), my_group, jnp.int32),
        coef,
        block_rows,
        block_cols,
        block_live,
        geometry,
        slab,
        split,
        groups,
        groups if shared else 1,
    )
    near = lax.all_to_all(
        near.reshape(-1, width // split), axes, split_axis=0, concat_axis=0, tiled=True
    )
    rows = inverse_transform(jnp.asarray(inverse), near, split, tm_count)
    rows = lax.all_to_all(
        rows.reshape(steps, width), "tm", split_axis=0, concat_axis=0, tiled=True
    )
    return return_to_elements(own, rows.reshape(tm_count, steps_local, width))


def solution(mesh):
    return jax.shard_map(
        per_device,
        mesh=mesh,
        in_specs=(P("tm", "elem"), P(None, "elem"), P("elem"), P("elem"), P(), P(), P()),
        out_specs=P("tm", "elem"),
        check_vma=False,
    )
```

```python
import functools
import math

import jax
import jax.numpy as jnp
import numpy as np
from jax import lax
from jax.experimental import pallas as pl
from jax.experimental.pallas import tpu as pltpu
from jax.sharding import PartitionSpec as P

FS = 4
CLUSTER = 128
LANES = 128
LOG_HALF = 0.6931471805599453
SOFTEN = 0.05
INV_STEP = 4.0
FOUR_PI = 4.0 * math.pi
LOW = 256
UNROLL = 4
F32 = jnp.float32
BF16 = jnp.bfloat16


def fit(func, high, degree):
    nodes = (np.cos((np.arange(600) + 0.5) / 600 * np.pi) + 1) * (high / 2)
    series = np.polynomial.chebyshev.Chebyshev.fit(
        nodes, func(nodes), degree, domain=[0, high]
    )
    return [float(v) for v in series.convert(kind=np.polynomial.Polynomial).coef]


SIN_HALF = fit(lambda u: np.sin(np.pi * np.sqrt(u)) / np.sqrt(u), 0.25, 3)
COS_HALF = fit(lambda u: np.cos(np.pi * np.sqrt(u)), 0.25, 4)
ARCTAN = fit(lambda u: np.arctan(np.sqrt(u)) / np.sqrt(u) / (2 * np.pi), 1.0, 9)


def poly(coefs, u):
    total = jnp.full_like(u, coefs[-1])
    for value in coefs[-2::-1]:
        total = total * u + value
    return total


def monic(coefs, u):
    total = u + coefs[-2] / coefs[-1]
    for value in coefs[-3::-1]:
        total = total * u + value / coefs[-1]
    return total


def transform_tables(steps, freqs):
    time_ids = np.arange(steps)
    levels = np.arange(freqs)
    phase = (levels[:, None] * time_ids[None, :] % steps) * (2.0 * np.pi / steps)
    decay = np.exp2(-time_ids / steps)
    forward = np.stack([np.cos(phase) * decay, -np.sin(phase) * decay])
    weight = np.where(levels == 0, 1.0, 2.0)[:, None] / (decay * steps)[None, :]
    inverse = np.stack([np.cos(phase) * weight, -np.sin(phase) * weight])
    return forward, inverse


def laplace_table(freqs, steps):
    angles = np.arange(freqs) * (2.0 * np.pi / steps)
    zeta = math.exp(-LOG_HALF / steps) * np.exp(1j * angles)
    delta = (1.0 - zeta) + 0.5 * (1.0 - zeta) ** 2
    return INV_STEP * delta


def packed_tables(steps, freqs, split):
    forward, inverse = transform_tables(steps, freqs)
    each = FS // split
    dests = freqs // each
    fwd = np.zeros((dests, 2, split, each, split, steps), np.float64)
    inv = np.zeros((dests, 2, split, each, split, steps), np.float64)
    for half in range(split):
        rows = forward.reshape(2, dests, each, steps).transpose(1, 0, 2, 3)
        fwd[:, :, half, :, half, :] = rows
        rows = inverse.reshape(2, dests, each, steps).transpose(1, 0, 2, 3)
        inv[:, :, half, :, half, :] = rows
    fwd = fwd.reshape(dests * 2 * FS, split * steps)
    inv = inv.reshape(dests * 2 * FS, split * steps).T
    return fwd.astype(np.float32), np.ascontiguousarray(inv).astype(np.float32)


def parts_of(x, count):
    out = []
    for _ in range(count - 1):
        head = x.astype(BF16).astype(F32)
        out.append(head)
        x = x - head
    return out + [x]


def one_hot_low(low_row):
    width = low_row.shape[1]
    ids = lax.broadcasted_iota(jnp.int32, (LOW, width), 0)
    return jnp.where(ids == low_row, 1.0, 0.0).astype(BF16)


def gather_body(own_ref, lhs_ref, high_count, chunk, emit):
    def step(c, _):
        at = pl.multiple_of(c * chunk, chunk)
        own = own_ref[:, pl.ds(at, chunk)]
        high = jnp.broadcast_to(own >> 8, (8, chunk))
        hot = one_hot_low(own & (LOW - 1))
        picked = jnp.dot(lhs_ref[...], hot, preferred_element_type=F32)
        top = jnp.zeros((8, chunk), F32)
        bottom = jnp.zeros((8, chunk), F32)
        for h in range(high_count):
            mask = high == h
            top += jnp.where(mask, picked[16 * h : 16 * h + 8], 0.0)
            bottom += jnp.where(mask, picked[16 * h + 8 : 16 * h + 16], 0.0)
        emit(c, top, bottom)
        return 0

    lax.fori_loop(0, own_ref.shape[1] // chunk, step, 0, unroll=UNROLL)


def order_history_kernel(own_ref, hist_ref, out_ref, lhs_ref):
    elems = own_ref.shape[1]
    width = out_ref.shape[2]
    chunk = min(256, width)
    for h in range(elems // LOW):
        pieces = parts_of(hist_ref[:, LOW * h : LOW * h + LOW], 2)
        lhs_ref[16 * h : 16 * h + 16, :] = jnp.concatenate(pieces, axis=0).astype(BF16)
    per = width // chunk

    def emit(c, top, bottom):
        at = pl.multiple_of(lax.rem(c, per) * chunk, chunk)
        out_ref[c // per, :, pl.ds(at, chunk)] = top + bottom

    gather_body(own_ref, lhs_ref, elems // LOW, chunk, emit)


def order_history(own, history, width):
    steps, elems = history.shape
    return pl.pallas_call(
        order_history_kernel,
        out_shape=jax.ShapeDtypeStruct((elems // width, steps, width), F32),
        scratch_shapes=[pltpu.VMEM((elems // LOW * 16, LOW), BF16)],
        name="order_history",
    )(own, history)


def order_geometry_kernel(own_ref, pts_ref, area_ref, out_ref, lhs_ref):
    elems = own_ref.shape[1]
    for h in range(elems // LOW):
        at = slice(LOW * h, LOW * h + LOW)
        rows = jnp.concatenate([pts_ref[:, at], area_ref[:, at] * (1.0 / FOUR_PI)], axis=0)
        pieces = parts_of(rows, 3) + [jnp.zeros_like(rows)]
        lhs_ref[16 * h : 16 * h + 16, :] = jnp.concatenate(pieces, axis=0).astype(BF16)

    def emit(c, top, bottom):
        total = top[0:4] + top[4:8] + bottom[0:4]
        total = jnp.concatenate([total, jnp.zeros_like(total)], axis=0)
        out_ref[2 * c] = total[:, :CLUSTER]
        out_ref[2 * c + 1] = total[:, CLUSTER:]

    gather_body(own_ref, lhs_ref, elems // LOW, 2 * CLUSTER, emit)


def order_geometry(own, points, areas):
    elems = own.shape[1]
    return pl.pallas_call(
        order_geometry_kernel,
        out_shape=jax.ShapeDtypeStruct((elems // CLUSTER, 8, CLUSTER), F32),
        scratch_shapes=[pltpu.VMEM((elems // LOW * 16, LOW), BF16)],
        name="order_geometry",
    )(own, points, areas)


def return_kernel(own_ref, near_ref, out_ref, lhs_ref, hot_ref, acc_ref):
    pieces_count, _, width = near_ref.shape
    elems = own_ref.shape[1]
    high_count = elems // LOW
    chunk = lhs_ref.shape[1]
    per = chunk // width
    acc_ref[...] = jnp.zeros_like(acc_ref)

    def step(c, _):
        at = pl.multiple_of(c * chunk, chunk)
        own = own_ref[:, pl.ds(at, chunk)]
        hot_ref[...] = one_hot_low(own & (LOW - 1))
        high = jnp.broadcast_to(own >> 8, (8, chunk))
        for p in range(per):
            lanes = slice(p * width, p * width + width)
            head, tail = parts_of(near_ref[c * per + p], 2)
            here = high[:, lanes]
            for h in range(high_count):
                mask = here == h
                both = [jnp.where(mask, head, 0.0), jnp.where(mask, tail, 0.0)]
                lhs_ref[16 * h : 16 * h + 16, lanes] = jnp.concatenate(both, axis=0).astype(BF16)
        acc_ref[...] += lax.dot_general(
            lhs_ref[...], hot_ref[...], (((1,), (1,)), ((), ())), preferred_element_type=F32
        )
        return 0

    lax.fori_loop(0, elems // chunk, step, 0)
    for h in range(high_count):
        out_ref[:, LOW * h : LOW * h + LOW] = (
            acc_ref[16 * h : 16 * h + 8, :] + acc_ref[16 * h + 8 : 16 * h + 16, :]
        )


def return_to_elements(own, values):
    pieces, steps, width = values.shape
    elems = own.shape[1]
    chunk = max(1024, width)
    return pl.pallas_call(
        return_kernel,
        out_shape=jax.ShapeDtypeStruct((steps, elems), F32),
        scratch_shapes=[
            pltpu.VMEM((elems // LOW * 16, chunk), BF16),
            pltpu.VMEM((LOW, chunk), BF16),
            pltpu.VMEM((elems // LOW * 16, LOW), F32),
        ],
        name="return_to_elements",
    )(own, values)


def forward_kernel(split, table_ref, x_ref, out_ref):
    steps, width = x_ref.shape
    half = width // split
    stacked = jnp.concatenate([x_ref[:, half * s : half * s + half] for s in range(split)], axis=0)
    out_ref[...] = jnp.dot(
        table_ref[...], stacked, precision=lax.Precision.HIGHEST, preferred_element_type=F32
    )


def forward_transform(table, x, split):
    return pl.pallas_call(
        functools.partial(forward_kernel, split),
        out_shape=jax.ShapeDtypeStruct((table.shape[0], x.shape[1] // split), F32),
        name="forward_transform",
    )(table, x)


def inverse_kernel(split, table_ref, x_ref, out_ref):
    total, half = x_ref.shape
    dests, steps_local, _ = out_ref.shape
    steps = dests * steps_local
    values = jnp.dot(
        table_ref[...], x_ref[...], precision=lax.Precision.HIGHEST, preferred_element_type=F32
    )
    for s in range(split):
        for d in range(dests):
            at = s * steps + d * steps_local
            out_ref[d, :, half * s : half * s + half] = values[at : at + steps_local]


def inverse_transform(table, x, split, dests):
    steps = table.shape[0] // split
    return pl.pallas_call(
        functools.partial(inverse_kernel, split),
        out_shape=jax.ShapeDtypeStruct((dests, steps // dests, x.shape[1] * split), F32),
        name="inverse_transform",
    )(table, x)


def near_kernel(
    cfg,
    meta,
    coef,
    rows,
    cols,
    live,
    geo_ref,
    val_ref,
    sel_ref,
    out_ref,
    acc_ref,
    col_ref,
    row_ref,
    buf_a,
    buf_b,
):
    each, split, groups, group_clusters, cap, own_groups, per_piece, feats = cfg
    clusters = geo_ref.shape[0]
    per_half = per_piece // split
    pieces = group_clusters // per_piece
    width = 3 + 2 * each
    acc_ref[...] = jnp.zeros_like(acc_ref)

    const_rows = sel_ref[0 : 3 * feats, 0 : 3 * LANES]

    def prepare(piece, _):
        for g in range(groups):
            index = piece * groups + g if own_groups == groups else g * pieces + piece
            chunk = val_ref[index]
            re, im = chunk[0:FS], chunk[FS : 2 * FS]
            ax, ay = jnp.abs(re), jnp.abs(im)
            large, small = jnp.maximum(ax, ay), jnp.minimum(ax, ay)
            q = small / jnp.maximum(large, 1e-37)
            turn = q * poly(ARCTAN, q * q)
            turn = jnp.where(ay > ax, 0.25 - turn, turn)
            turn = jnp.where(re < 0, 0.5 - turn, turn)
            turn = jnp.where(im < 0, -turn, turn)
            size = large * jnp.sqrt(1.0 + q * q)
            for w in range(per_piece):
                c = g * group_clusters + piece * per_piece + w
                half, lane = w // per_half, (w % per_half) * LANES
                mine = slice(half * each, half * each + each)
                place = geo_ref[c]
                coords = place[0:3]
                found = [
                    coords,
                    turn[mine, lane : lane + LANES],
                    size[mine, lane : lane + LANES] * place[3:4],
                ]
                if feats > width:
                    found.append(jnp.zeros((feats - width, LANES), F32))
                feature = jnp.concatenate(found, axis=0)
                pieces3 = parts_of(feature, 3)
                ones = jnp.ones((feats, LANES), F32)
                stacked = jnp.concatenate(pieces3 + [ones], axis=0)
                col_ref[c] = stacked.T.astype(BF16)
                lines = []
                for part in range(3):
                    x3 = pieces3[part]
                    lines.append(jnp.concatenate([-x3[k : k + 1] for k in range(3)], axis=1))
                lines.append(jnp.zeros((feats - 3, 3 * LANES), F32))
                tail = jnp.concatenate(lines, axis=0)
                row_ref[c] = jnp.concatenate([const_rows, tail], axis=0).astype(BF16)
        return 0

    lax.fori_loop(0, pieces, prepare, 0)

    decay = [coef[f] for f in range(each)]
    turns = [coef[each + f] for f in range(each)]
    sel = sel_ref[:, 3 * LANES :].astype(BF16)
    lives = [live[g if own_groups == groups else meta[0]] for g in range(own_groups)]
    total_live = sum(lives)
    idle = own_groups * group_clusters

    def locate(b):
        slot, inside = jnp.int32(0), b
        for g in range(1, own_groups):
            over = inside >= lives[g - 1]
            moved = jnp.logical_and(over, slot == g - 1)
            inside = jnp.where(moved, inside - lives[g - 1], inside)
            slot = jnp.where(moved, g, slot)
        valid = b < total_live
        slot = jnp.where(valid, slot, 0)
        inside = jnp.where(valid, inside, 0)
        group = slot if own_groups == groups else meta[0]
        at = group * cap + inside
        row = rows[at]
        target = jnp.where(valid, slot * group_clusters + row, idle)
        return group * group_clusters + row, cols[at], target

    def load(b, buf):
        row, col, _ = locate(b)
        left = col_ref[col]
        right = jnp.concatenate([row_ref[row], sel], axis=1)
        buf[...] = jnp.dot(left, right, preferred_element_type=F32)

    def work(b, buf):
        _, _, target = locate(b)
        sums = [jnp.zeros((8, LANES), F32) for _ in range(3 * each)]
        for j in range(CLUSTER // 8):
            lane = lambda k: buf[8 * j : 8 * j + 8, LANES * k : LANES * k + LANES]
            dx, dy, dz = lane(0), lane(1), lane(2)
            square = dx * dx + dy * dy + dz * dz + SOFTEN * SOFTEN
            inv = lax.rsqrt(square)
            dist = square * inv
            for f in range(each):
                weight = jnp.exp2(decay[f] * dist) * (inv * lane(3 + each + f))
                t = lane(3 + f) - turns[f] * dist
                t = t - jnp.round(t)
                u = t * t
                s = t * monic(SIN_HALF, u)
                ws = weight * s
                sums[3 * f] += weight
                sums[3 * f + 1] += ws * s
                sums[3 * f + 2] += ws * monic(COS_HALF, u)
        for f in range(each):
            whole, squared, mixed = sums[3 * f : 3 * f + 3]
            acc_ref[target, f] += whole - (2.0 * SIN_HALF[-1] ** 2) * squared
            acc_ref[target, each + f] += (2.0 * SIN_HALF[-1] * COS_HALF[-1]) * mixed

    load(jnp.int32(0), buf_a)
    load(jnp.int32(1), buf_b)

    def pair(i, _):
        work(2 * i, buf_a)
        load(2 * i + 2, buf_a)
        work(2 * i + 1, buf_b)
        load(2 * i + 3, buf_b)
        return 0

    lax.fori_loop(0, (total_live + 1) // 2, pair, 0)

    def finish(piece, _):
        for slot in range(own_groups):
            for w in range(per_piece):
                c = slot * group_clusters + piece * per_piece + w
                half, lane = w // per_half, (w % per_half) * LANES
                total = jnp.sum(acc_ref[c], axis=1)
                dest = piece * own_groups + slot
                for part in range(2):
                    first = part * FS + half * each
                    out_ref[dest, first : first + each, lane : lane + LANES] = total[
                        part * each : part * each + each
                    ]
        return 0

    lax.fori_loop(0, pieces, finish, 0)


def near_field(meta, coef, rows, cols, live, geometry, values, split, groups, own_groups):
    each = FS // split
    clusters = geometry.shape[0]
    group_clusters = clusters // groups
    per_piece = values.shape[2] // LANES * split
    feats = -(-(3 + 2 * each) // 8) * 8
    width = 3 + 2 * each
    sel = np.zeros((4 * feats, width, LANES), np.float32)
    for part in range(3):
        for k in range(width):
            sel[part * feats + k, k] = 1.0
    sel = sel.reshape(4 * feats, width * LANES)
    cfg = (
        each,
        split,
        groups,
        group_clusters,
        rows.shape[0] // groups,
        own_groups,
        per_piece,
        feats,
    )
    smem = pl.BlockSpec(memory_space=pltpu.SMEM)
    vmem = pl.BlockSpec(memory_space=pltpu.VMEM)
    dests = own_groups * group_clusters // per_piece
    return pl.pallas_call(
        functools.partial(near_kernel, cfg),
        out_shape=jax.ShapeDtypeStruct((dests, 2 * FS, per_piece // split * LANES), F32),
        in_specs=[smem] * 5 + [vmem] * 3,
        out_specs=vmem,
        scratch_shapes=[
            pltpu.VMEM((own_groups * group_clusters + 1, 2 * each, 8, LANES), F32),
            pltpu.VMEM((clusters, CLUSTER, 4 * feats), BF16),
            pltpu.VMEM((clusters, 4 * feats, 3 * LANES), BF16),
            pltpu.VMEM((CLUSTER, width * LANES), F32),
            pltpu.VMEM((CLUSTER, width * LANES), F32),
        ],
        compiler_params=pltpu.CompilerParams(vmem_limit_bytes=56 * 2**20),
        name="near_field",
    )(meta, coef, rows, cols, live, geometry, values, jnp.asarray(sel))


def per_device(history, points, areas, ownership, block_rows, block_cols, block_live):
    steps_local, elem_local = history.shape
    tm_count = lax.axis_size("tm")
    groups = lax.axis_size("elem")
    steps = steps_local * tm_count
    freqs = FS * tm_count
    width = elem_local // tm_count
    split = groups if groups == 2 and width % (2 * LANES) == 0 else 1
    each = FS // split
    shared = split == groups
    axes = ("tm", "elem") if shared else "tm"
    forward, inverse = packed_tables(steps, freqs, split)
    lap = laplace_table(freqs, steps).reshape(-1, each)
    coefs = np.concatenate([-lap.real / LOG_HALF, lap.imag / (2.0 * np.pi)], axis=1)
    my_group = lax.axis_index("elem")
    mine = lax.axis_index("tm") * split + (my_group if shared else 0)
    coef = lax.dynamic_index_in_dim(jnp.asarray(coefs.astype(np.float32)), mine, 0, keepdims=False)

    own = ownership.reshape(1, elem_local)
    pieces = order_history(own, history, width)
    by_time = lax.all_to_all(
        pieces.reshape(tm_count * steps_local, width), "tm", split_axis=0, concat_axis=0, tiled=True
    )
    geometry = order_geometry(own, points, areas.reshape(1, elem_local))
    geometry = lax.all_gather(geometry, "elem", axis=0, tiled=True)
    spectra = forward_transform(jnp.asarray(forward), by_time, split)
    slab = lax.all_to_all(spectra, axes, split_axis=0, concat_axis=0, tiled=True)
    if not shared:
        slab = lax.all_gather(slab, "elem", axis=0, tiled=True)
    slab = slab.reshape(-1, 2 * FS, width // split)
    near = near_field(
        jnp.full((1,), my_group, jnp.int32),
        coef,
        block_rows,
        block_cols,
        block_live,
        geometry,
        slab,
        split,
        groups,
        groups if shared else 1,
    )
    near = lax.all_to_all(
        near.reshape(-1, width // split), axes, split_axis=0, concat_axis=0, tiled=True
    )
    rows = inverse_transform(jnp.asarray(inverse), near, split, tm_count)
    rows = lax.all_to_all(
        rows.reshape(steps, width), "tm", split_axis=0, concat_axis=0, tiled=True
    )
    return return_to_elements(own, rows.reshape(tm_count, steps_local, width))


def solution(mesh):
    return jax.shard_map(
        per_device,
        mesh=mesh,
        in_specs=(P("tm", "elem"), P(None, "elem"), P("elem"), P("elem"), P(), P(), P()),
        out_specs=P("tm", "elem"),
        check_vma=False,
    )
```

```python
import functools
import math

import jax
import jax.numpy as jnp
import numpy as np
from jax import lax
from jax.experimental import pallas as pl
from jax.experimental.pallas import tpu as pltpu
from jax.sharding import PartitionSpec as P

FS = 4
CLUSTER = 128
LANES = 128
LOG_HALF = 0.6931471805599453
SOFTEN = 0.05
INV_STEP = 4.0
FOUR_PI = 4.0 * math.pi
LOW = 256
UNROLL = 4
F32 = jnp.float32
BF16 = jnp.bfloat16


def fit(func, high, degree):
    nodes = (np.cos((np.arange(600) + 0.5) / 600 * np.pi) + 1) * (high / 2)
    series = np.polynomial.chebyshev.Chebyshev.fit(
        nodes, func(nodes), degree, domain=[0, high]
    )
    return [float(v) for v in series.convert(kind=np.polynomial.Polynomial).coef]


SIN_HALF = fit(lambda u: np.sin(np.pi * np.sqrt(u)) / np.sqrt(u), 0.25, 3)
COS_HALF = fit(lambda u: np.cos(np.pi * np.sqrt(u)), 0.25, 4)
ARCTAN = fit(lambda u: np.arctan(np.sqrt(u)) / np.sqrt(u) / (2 * np.pi), 1.0, 9)


def poly(coefs, u):
    total = jnp.full_like(u, coefs[-1])
    for value in coefs[-2::-1]:
        total = total * u + value
    return total


def monic(coefs, u):
    total = u + coefs[-2] / coefs[-1]
    for value in coefs[-3::-1]:
        total = total * u + value / coefs[-1]
    return total


def transform_tables(steps, freqs):
    time_ids = np.arange(steps)
    levels = np.arange(freqs)
    phase = (levels[:, None] * time_ids[None, :] % steps) * (2.0 * np.pi / steps)
    decay = np.exp2(-time_ids / steps)
    forward = np.stack([np.cos(phase) * decay, -np.sin(phase) * decay])
    weight = np.where(levels == 0, 1.0, 2.0)[:, None] / (decay * steps)[None, :]
    inverse = np.stack([np.cos(phase) * weight, -np.sin(phase) * weight])
    return forward, inverse


def laplace_table(freqs, steps):
    angles = np.arange(freqs) * (2.0 * np.pi / steps)
    zeta = math.exp(-LOG_HALF / steps) * np.exp(1j * angles)
    delta = (1.0 - zeta) + 0.5 * (1.0 - zeta) ** 2
    return INV_STEP * delta


def packed_tables(steps, freqs, split):
    forward, inverse = transform_tables(steps, freqs)
    each = FS // split
    dests = freqs // each
    fwd = np.zeros((dests, 2, split, each, split, steps), np.float64)
    inv = np.zeros((dests, 2, split, each, split, steps), np.float64)
    for half in range(split):
        rows = forward.reshape(2, dests, each, steps).transpose(1, 0, 2, 3)
        fwd[:, :, half, :, half, :] = rows
        rows = inverse.reshape(2, dests, each, steps).transpose(1, 0, 2, 3)
        inv[:, :, half, :, half, :] = rows
    fwd = fwd.reshape(dests * 2 * FS, split * steps)
    inv = inv.reshape(dests * 2 * FS, split * steps).T
    return fwd.astype(np.float32), np.ascontiguousarray(inv).astype(np.float32)


def held(x):
    return pltpu.with_memory_space_constraint(x, pltpu.VMEM)


def parts_of(x, count):
    out = []
    for _ in range(count - 1):
        head = x.astype(BF16).astype(F32)
        out.append(head)
        x = x - head
    return out + [x]


def one_hot_low(low_row):
    width = low_row.shape[1]
    ids = lax.broadcasted_iota(jnp.int32, (LOW, width), 0)
    return jnp.where(ids == low_row, 1.0, 0.0).astype(BF16)


def stack_parts(read, count, rows, high_count, lhs_ref):
    group = 16 // rows
    for h in range(0, high_count, group):
        pieces = [parts_of(read(h + i), count) for i in range(group)]
        for part in range(count):
            block = jnp.concatenate([piece[part] for piece in pieces], axis=0)
            lhs_ref[h * rows : h * rows + 16, part * LOW : part * LOW + LOW] = block.astype(BF16)


def gather_body(own_ref, lhs_ref, rows, chunk, emit):
    count = lhs_ref.shape[1] // LOW
    each = 8 // rows

    def step(c, _):
        at = pl.multiple_of(c * chunk, chunk)
        own = own_ref[:, pl.ds(at, chunk)]
        high = jnp.broadcast_to(own >> 8, (8, chunk))
        if each > 1:
            high = high - lax.broadcasted_iota(jnp.int32, (8, chunk), 0) // rows
        hot = one_hot_low(own & (LOW - 1))
        picked = jnp.dot(
            lhs_ref[...], jnp.concatenate([hot] * count, axis=0), preferred_element_type=F32
        )
        total = jnp.zeros((8, chunk), F32)
        for v in range(picked.shape[0] // 8):
            total += jnp.where(high == v * each, picked[8 * v : 8 * v + 8], 0.0)
        emit(c, total)
        return 0

    lax.fori_loop(0, own_ref.shape[1] // chunk, step, 0, unroll=UNROLL)


def order_history_kernel(own_ref, hist_ref, out_ref, lhs_ref):
    elems = own_ref.shape[1]
    width = out_ref.shape[2]
    chunk = min(256, width)
    stack_parts(
        lambda h: hist_ref[:, LOW * h : LOW * h + LOW], 2, 8, elems // LOW, lhs_ref
    )
    per = width // chunk

    def emit(c, total):
        at = pl.multiple_of(lax.rem(c, per) * chunk, chunk)
        out_ref[c // per, :, pl.ds(at, chunk)] = total

    gather_body(own_ref, lhs_ref, 8, chunk, emit)


def order_history(own, history, width):
    steps, elems = history.shape
    return pl.pallas_call(
        order_history_kernel,
        out_shape=pltpu.VMEM((elems // width, steps, width), F32),
        scratch_shapes=[pltpu.VMEM((elems // LOW * 8, 2 * LOW), BF16)],
        name="order_history",
    )(own, history)


def order_geometry_kernel(own_ref, pts_ref, area_ref, out_ref, lhs_ref):
    elems = own_ref.shape[1]

    def read(h):
        at = slice(LOW * h, LOW * h + LOW)
        return jnp.concatenate([pts_ref[:, at], area_ref[:, at] * (1.0 / FOUR_PI)], axis=0)

    stack_parts(read, 3, 4, elems // LOW, lhs_ref)

    def emit(c, total):
        total = total + pltpu.roll(total, 4, 0)
        out_ref[2 * c] = total[:, :CLUSTER]
        out_ref[2 * c + 1] = total[:, CLUSTER:]

    gather_body(own_ref, lhs_ref, 4, 2 * CLUSTER, emit)


def order_geometry(own, points, areas):
    elems = own.shape[1]
    return pl.pallas_call(
        order_geometry_kernel,
        out_shape=jax.ShapeDtypeStruct((elems // CLUSTER, 8, CLUSTER), F32),
        scratch_shapes=[pltpu.VMEM((elems // LOW * 4, 3 * LOW), BF16)],
        name="order_geometry",
    )(own, points, areas)


def return_kernel(own_ref, near_ref, out_ref, lhs_ref, hot_ref, acc_ref):
    width = near_ref.shape[2]
    elems = own_ref.shape[1]
    high_count = elems // LOW
    chunk = lhs_ref.shape[1] // 2
    per = chunk // width
    acc_ref[...] = jnp.zeros_like(acc_ref)

    def step(c, _):
        at = pl.multiple_of(c * chunk, chunk)
        own = own_ref[:, pl.ds(at, chunk)]
        hot = one_hot_low(own & (LOW - 1))
        hot_ref[:, :chunk] = hot
        hot_ref[:, chunk:] = hot
        high = jnp.broadcast_to(own >> 8, (8, chunk))
        for p in range(per):
            lanes = slice(p * width, p * width + width)
            pieces = parts_of(near_ref[c * per + p], 2)
            here = high[:, lanes]
            for h in range(0, high_count, 2):
                for part, piece in enumerate(pieces):
                    both = [jnp.where(here == h + i, piece, 0.0) for i in range(2)]
                    to = slice(part * chunk + p * width, part * chunk + p * width + width)
                    lhs_ref[8 * h : 8 * h + 16, to] = jnp.concatenate(both, axis=0).astype(BF16)
        acc_ref[...] += lax.dot_general(
            lhs_ref[...], hot_ref[...], (((1,), (1,)), ((), ())), preferred_element_type=F32
        )
        return 0

    lax.fori_loop(0, elems // chunk, step, 0)
    for h in range(high_count):
        out_ref[:, LOW * h : LOW * h + LOW] = acc_ref[8 * h : 8 * h + 8, :]


def return_to_elements(own, values):
    pieces, steps, width = values.shape
    elems = own.shape[1]
    chunk = max(1024, width)
    return pl.pallas_call(
        return_kernel,
        out_shape=jax.ShapeDtypeStruct((steps, elems), F32),
        scratch_shapes=[
            pltpu.VMEM((elems // LOW * 8, 2 * chunk), BF16),
            pltpu.VMEM((LOW, 2 * chunk), BF16),
            pltpu.VMEM((elems // LOW * 8, LOW), F32),
        ],
        name="return_to_elements",
    )(held(own), held(values))


def forward_kernel(split, table_ref, x_ref, out_ref):
    steps, width = x_ref.shape
    half = width // split
    stacked = jnp.concatenate([x_ref[:, half * s : half * s + half] for s in range(split)], axis=0)
    out_ref[...] = jnp.dot(
        table_ref[...], stacked, precision=lax.Precision.HIGHEST, preferred_element_type=F32
    )


def forward_transform(table, x, split):
    return pl.pallas_call(
        functools.partial(forward_kernel, split),
        out_shape=pltpu.VMEM((table.shape[0], x.shape[1] // split), F32),
        name="forward_transform",
    )(held(table), held(x))


def inverse_kernel(split, table_ref, x_ref, out_ref):
    total, half = x_ref.shape
    dests, steps_local, _ = out_ref.shape
    steps = dests * steps_local
    values = jnp.dot(
        table_ref[...], x_ref[...], precision=lax.Precision.HIGHEST, preferred_element_type=F32
    )
    for s in range(split):
        for d in range(dests):
            at = s * steps + d * steps_local
            out_ref[d, :, half * s : half * s + half] = values[at : at + steps_local]


def inverse_transform(table, x, split, dests):
    steps = table.shape[0] // split
    return pl.pallas_call(
        functools.partial(inverse_kernel, split),
        out_shape=pltpu.VMEM((dests, steps // dests, x.shape[1] * split), F32),
        name="inverse_transform",
    )(held(table), held(x))


def near_kernel(
    cfg,
    coef,
    rows,
    cols,
    live,
    geo_ref,
    val_ref,
    sel_ref,
    out_ref,
    acc_ref,
    col_ref,
    row_ref,
    buf_a,
    buf_b,
):
    each, split, groups, group_clusters, cap, own_groups, per_piece, feats = cfg
    my_group = lax.axis_index("elem")
    mine = lax.axis_index("tm")
    if own_groups == groups:
        mine = mine * split + my_group
    clusters = geo_ref.shape[0]
    per_half = per_piece // split
    pieces = group_clusters // per_piece
    width = 3 + 2 * each
    acc_ref[...] = jnp.zeros_like(acc_ref)

    const_rows = sel_ref[0 : 3 * feats, 0 : 3 * LANES]

    def prepare(piece, _):
        for g in range(groups):
            index = piece * groups + g if own_groups == groups else g * pieces + piece
            chunk = val_ref[index]
            re, im = chunk[0:FS], chunk[FS : 2 * FS]
            ax, ay = jnp.abs(re), jnp.abs(im)
            large, small = jnp.maximum(ax, ay), jnp.minimum(ax, ay)
            q = small / jnp.maximum(large, 1e-37)
            turn = q * poly(ARCTAN, q * q)
            turn = jnp.where(ay > ax, 0.25 - turn, turn)
            turn = jnp.where(re < 0, 0.5 - turn, turn)
            turn = jnp.where(im < 0, -turn, turn)
            size = large * jnp.sqrt(1.0 + q * q)
            for w in range(per_piece):
                c = g * group_clusters + piece * per_piece + w
                half, lane = w // per_half, (w % per_half) * LANES
                mine = slice(half * each, half * each + each)
                place = geo_ref[c]
                coords = place[0:3]
                found = [
                    coords,
                    turn[mine, lane : lane + LANES],
                    size[mine, lane : lane + LANES] * place[3:4],
                ]
                if feats > width:
                    found.append(jnp.zeros((feats - width, LANES), F32))
                feature = jnp.concatenate(found, axis=0)
                pieces3 = parts_of(feature, 3)
                ones = jnp.ones((feats, LANES), F32)
                stacked = jnp.concatenate(pieces3 + [ones], axis=0)
                col_ref[c] = stacked.T.astype(BF16)
                lines = []
                for part in range(3):
                    x3 = pieces3[part]
                    lines.append(jnp.concatenate([-x3[k : k + 1] for k in range(3)], axis=1))
                lines.append(jnp.zeros((feats - 3, 3 * LANES), F32))
                tail = jnp.concatenate(lines, axis=0)
                row_ref[c] = jnp.concatenate([const_rows, tail], axis=0).astype(BF16)
        return 0

    lax.fori_loop(0, pieces, prepare, 0)

    decay = [coef[mine * 2 * each + f] for f in range(each)]
    turns = [coef[mine * 2 * each + each + f] for f in range(each)]
    sel = sel_ref[:, 3 * LANES :].astype(BF16)
    lives = [live[g if own_groups == groups else my_group] for g in range(own_groups)]
    total_live = sum(lives)
    idle = own_groups * group_clusters

    def locate(b):
        slot, inside = jnp.int32(0), b
        for g in range(1, own_groups):
            over = inside >= lives[g - 1]
            moved = jnp.logical_and(over, slot == g - 1)
            inside = jnp.where(moved, inside - lives[g - 1], inside)
            slot = jnp.where(moved, g, slot)
        valid = b < total_live
        slot = jnp.where(valid, slot, 0)
        inside = jnp.where(valid, inside, 0)
        group = slot if own_groups == groups else my_group
        at = group * cap + inside
        row = rows[at]
        target = jnp.where(valid, slot * group_clusters + row, idle)
        return group * group_clusters + row, cols[at], target

    def load(b, buf):
        row, col, _ = locate(b)
        left = col_ref[col]
        right = jnp.concatenate([row_ref[row], sel], axis=1)
        buf[...] = jnp.dot(left, right, preferred_element_type=F32)

    def work(b, buf):
        _, _, target = locate(b)
        sums = [jnp.zeros((8, LANES), F32) for _ in range(3 * each)]
        for j in range(CLUSTER // 8):
            lane = lambda k: buf[8 * j : 8 * j + 8, LANES * k : LANES * k + LANES]
            dx, dy, dz = lane(0), lane(1), lane(2)
            square = dx * dx + dy * dy + dz * dz + SOFTEN * SOFTEN
            inv = lax.rsqrt(square)
            dist = square * inv
            for f in range(each):
                weight = jnp.exp2(decay[f] * dist) * (inv * lane(3 + each + f))
                t = lane(3 + f) - turns[f] * dist
                t = t - jnp.round(t)
                u = t * t
                s = t * monic(SIN_HALF, u)
                ws = weight * s
                sums[3 * f] += weight
                sums[3 * f + 1] += ws * s
                sums[3 * f + 2] += ws * monic(COS_HALF, u)
        for f in range(each):
            whole, squared, mixed = sums[3 * f : 3 * f + 3]
            acc_ref[target, f] += whole - (2.0 * SIN_HALF[-1] ** 2) * squared
            acc_ref[target, each + f] += (2.0 * SIN_HALF[-1] * COS_HALF[-1]) * mixed

    load(jnp.int32(0), buf_a)
    load(jnp.int32(1), buf_b)

    def pair(i, _):
        for q in range(0, 4, 2):
            work(4 * i + q, buf_a)
            load(4 * i + q + 2, buf_a)
            work(4 * i + q + 1, buf_b)
            load(4 * i + q + 3, buf_b)
        return 0

    lax.fori_loop(0, (total_live + 3) // 4, pair, 0)

    def finish(piece, _):
        for slot in range(own_groups):
            for w in range(per_piece):
                c = slot * group_clusters + piece * per_piece + w
                half, lane = w // per_half, (w % per_half) * LANES
                total = jnp.sum(acc_ref[c], axis=1)
                dest = piece * own_groups + slot
                for part in range(2):
                    first = part * FS + half * each
                    out_ref[dest, first : first + each, lane : lane + LANES] = total[
                        part * each : part * each + each
                    ]
        return 0

    lax.fori_loop(0, pieces, finish, 0)


def near_field(coef, rows, cols, live, geometry, values, split, groups, own_groups):
    each = FS // split
    clusters = geometry.shape[0]
    group_clusters = clusters // groups
    per_piece = values.shape[2] // LANES * split
    feats = -(-(3 + 2 * each) // 8) * 8
    width = 3 + 2 * each
    sel = np.zeros((4 * feats, width, LANES), np.float32)
    for part in range(3):
        for k in range(width):
            sel[part * feats + k, k] = 1.0
    sel = sel.reshape(4 * feats, width * LANES)
    cfg = (
        each,
        split,
        groups,
        group_clusters,
        rows.shape[0] // groups,
        own_groups,
        per_piece,
        feats,
    )
    smem = pl.BlockSpec(memory_space=pltpu.SMEM)
    vmem = pl.BlockSpec(memory_space=pltpu.VMEM)
    dests = own_groups * group_clusters // per_piece
    return pl.pallas_call(
        functools.partial(near_kernel, cfg),
        out_shape=pltpu.VMEM((dests, 2 * FS, per_piece // split * LANES), F32),
        in_specs=[smem] * 4 + [vmem] * 3,
        out_specs=vmem,
        scratch_shapes=[
            pltpu.VMEM((own_groups * group_clusters + 1, 2 * each, 8, LANES), F32),
            pltpu.VMEM((clusters, CLUSTER, 4 * feats), BF16),
            pltpu.VMEM((clusters, 4 * feats, 3 * LANES), BF16),
            pltpu.VMEM((CLUSTER, width * LANES), F32),
            pltpu.VMEM((CLUSTER, width * LANES), F32),
        ],
        compiler_params=pltpu.CompilerParams(vmem_limit_bytes=56 * 2**20),
        name="near_field",
    )(coef, rows, cols, live, held(geometry), held(values), held(jnp.asarray(sel)))


def per_device(history, points, areas, ownership, block_rows, block_cols, block_live):
    steps_local, elem_local = history.shape
    tm_count = lax.axis_size("tm")
    groups = lax.axis_size("elem")
    steps = steps_local * tm_count
    freqs = FS * tm_count
    width = elem_local // tm_count
    split = groups if groups == 2 and width % (2 * LANES) == 0 else 1
    each = FS // split
    shared = split == groups
    axes = ("tm", "elem") if shared else "tm"
    forward, inverse = packed_tables(steps, freqs, split)
    lap = laplace_table(freqs, steps).reshape(-1, each)
    coefs = np.concatenate([-lap.real / LOG_HALF, lap.imag / (2.0 * np.pi)], axis=1)
    coef = jnp.asarray(coefs.astype(np.float32).reshape(-1))

    own = ownership.reshape(1, elem_local)
    pieces = order_history(own, history, width)
    by_time = lax.all_to_all(
        pieces.reshape(tm_count * steps_local, width), "tm", split_axis=0, concat_axis=0, tiled=True
    )
    geometry = order_geometry(own, points, areas.reshape(1, elem_local))
    geometry = lax.all_gather(geometry, "elem", axis=0, tiled=True)
    spectra = forward_transform(jnp.asarray(forward), by_time, split)
    slab = lax.all_to_all(spectra, axes, split_axis=0, concat_axis=0, tiled=True)
    if not shared:
        slab = lax.all_gather(slab, "elem", axis=0, tiled=True)
    slab = slab.reshape(-1, 2 * FS, width // split)
    near = near_field(
        coef,
        block_rows,
        block_cols,
        block_live,
        geometry,
        slab,
        split,
        groups,
        groups if shared else 1,
    )
    near = lax.all_to_all(
        near.reshape(-1, width // split), axes, split_axis=0, concat_axis=0, tiled=True
    )
    rows = inverse_transform(jnp.asarray(inverse), near, split, tm_count)
    rows = lax.all_to_all(
        rows.reshape(steps, width), "tm", split_axis=0, concat_axis=0, tiled=True
    )
    return return_to_elements(own, rows.reshape(tm_count, steps_local, width))


def solution(mesh):
    return jax.shard_map(
        per_device,
        mesh=mesh,
        in_specs=(P("tm", "elem"), P(None, "elem"), P("elem"), P("elem"), P(), P(), P()),
        out_specs=P("tm", "elem"),
        check_vma=False,
    )
```

```python
import functools
import math

import jax
import jax.numpy as jnp
import numpy as np
from jax import lax
from jax.experimental import pallas as pl
from jax.experimental.pallas import tpu as pltpu
from jax.sharding import PartitionSpec as P

FS = 4
CLUSTER = 128
LANES = 128
LOG_HALF = 0.6931471805599453
SOFTEN = 0.05
INV_STEP = 4.0
FOUR_PI = 4.0 * math.pi
LOW = 256
GRID = 64
TERMS = 48
UNROLL = 4
F32 = jnp.float32
BF16 = jnp.bfloat16


def fit(func, high, degree):
    nodes = (np.cos((np.arange(600) + 0.5) / 600 * np.pi) + 1) * (high / 2)
    series = np.polynomial.chebyshev.Chebyshev.fit(
        nodes, func(nodes), degree, domain=[0, high]
    )
    return [float(v) for v in series.convert(kind=np.polynomial.Polynomial).coef]


SIN_QUARTER = fit(lambda u: np.sin(np.pi / 2 * np.sqrt(u)) / np.sqrt(u), 0.25, 2)
COS_QUARTER = fit(lambda u: np.cos(np.pi / 2 * np.sqrt(u)), 0.25, 3)
HALF_SIN = 2.0 * SIN_QUARTER[-1] * COS_QUARTER[-1]
HALF_COS = 2.0 * SIN_QUARTER[-1] ** 2
ARCTAN = fit(lambda u: np.arctan(np.sqrt(u)) / np.sqrt(u) / (2 * np.pi), 1.0, 9)


def poly(coefs, u):
    total = jnp.full_like(u, coefs[-1])
    for value in coefs[-2::-1]:
        total = total * u + value
    return total


def monic(coefs, u):
    total = u + coefs[-2] / coefs[-1]
    for value in coefs[-3::-1]:
        total = total * u + value / coefs[-1]
    return total


def transform_tables(steps, freqs):
    time_ids = np.arange(steps)
    levels = np.arange(freqs)
    phase = (levels[:, None] * time_ids[None, :] % steps) * (2.0 * np.pi / steps)
    decay = np.exp2(-time_ids / steps)
    forward = np.stack([np.cos(phase) * decay, -np.sin(phase) * decay])
    weight = np.where(levels == 0, 1.0, 2.0)[:, None] / (decay * steps)[None, :]
    inverse = np.stack([np.cos(phase) * weight, -np.sin(phase) * weight])
    return forward, inverse


def laplace_table(freqs, steps):
    angles = np.arange(freqs) * (2.0 * np.pi / steps)
    zeta = math.exp(-LOG_HALF / steps) * np.exp(1j * angles)
    delta = (1.0 - zeta) + 0.5 * (1.0 - zeta) ** 2
    return INV_STEP * delta


def packed_tables(steps, freqs, split):
    forward, inverse = transform_tables(steps, freqs)
    each = FS // split
    dests = freqs // each
    fwd = np.zeros((dests, 2, split, each, split, steps), np.float64)
    inv = np.zeros((dests, 2, split, each, split, steps), np.float64)
    for half in range(split):
        rows = forward.reshape(2, dests, each, steps).transpose(1, 0, 2, 3)
        fwd[:, :, half, :, half, :] = rows
        rows = inverse.reshape(2, dests, each, steps).transpose(1, 0, 2, 3)
        inv[:, :, half, :, half, :] = rows
    fwd = fwd.reshape(dests * 2 * FS, split * steps)
    inv = inv.reshape(dests * 2 * FS, split * steps).T
    return fwd.astype(np.float32), np.ascontiguousarray(inv).astype(np.float32)


def held(x):
    return pltpu.with_memory_space_constraint(x, pltpu.VMEM)


def outside(x):
    return pltpu.with_memory_space_constraint(x, pltpu.HBM)


def parts_of(x, count):
    out = []
    for _ in range(count - 1):
        head = x.astype(BF16).astype(F32)
        out.append(head)
        x = x - head
    return out + [x]


def one_hot_low(low_row):
    width = low_row.shape[1]
    ids = lax.broadcasted_iota(jnp.int32, (LOW, width), 0)
    return jnp.where(ids == low_row, 1.0, 0.0).astype(BF16)


def stack_parts(read, count, rows, high_count, lhs_ref):
    group = 16 // rows
    for h in range(0, high_count, group):
        pieces = [parts_of(read(h + i), count) for i in range(group)]
        for part in range(count):
            block = jnp.concatenate([piece[part] for piece in pieces], axis=0)
            lhs_ref[h * rows : h * rows + 16, part * LOW : part * LOW + LOW] = block.astype(BF16)


def gather_body(own_ref, lhs_ref, rows, chunk, emit):
    count = lhs_ref.shape[1] // LOW
    each = 8 // rows
    stride = 16 if each == 1 else 8

    def step(c, _):
        at = pl.multiple_of(c * chunk, chunk)
        own = own_ref[:, pl.ds(at, chunk)]
        high = jnp.broadcast_to(own >> 8, (8, chunk))
        if each > 1:
            high = high - lax.broadcasted_iota(jnp.int32, (8, chunk), 0) // rows
        hot = one_hot_low(own & (LOW - 1))
        picked = jnp.dot(
            lhs_ref[...], jnp.concatenate([hot] * count, axis=0), preferred_element_type=F32
        )
        total = jnp.zeros((8, chunk), F32)
        for v in range(picked.shape[0] // stride):
            value = picked[stride * v : stride * v + 8]
            if stride == 16:
                value = value + picked[16 * v + 8 : 16 * v + 16]
            total += jnp.where(high == v * each, value, 0.0)
        emit(c, total)
        return 0

    lax.fori_loop(0, own_ref.shape[1] // chunk, step, 0, unroll=UNROLL)


def order_history_kernel(own_ref, hist_ref, out_ref, lhs_ref):
    elems = own_ref.shape[1]
    width = out_ref.shape[2]
    chunk = min(256, width)
    for h in range(elems // LOW):
        pieces = parts_of(hist_ref[:, LOW * h : LOW * h + LOW], 2)
        lhs_ref[16 * h : 16 * h + 16, :] = jnp.concatenate(pieces, axis=0).astype(BF16)
    per = width // chunk

    def emit(c, total):
        at = pl.multiple_of(lax.rem(c, per) * chunk, chunk)
        out_ref[c // per, :, pl.ds(at, chunk)] = total

    gather_body(own_ref, lhs_ref, 8, chunk, emit)


def order_history(own, history, width):
    steps, elems = history.shape
    return pl.pallas_call(
        order_history_kernel,
        out_shape=pltpu.VMEM((elems // width, steps, width), F32),
        scratch_shapes=[pltpu.VMEM((elems // LOW * 16, LOW), BF16)],
        name="order_history",
    )(outside(own), outside(history))


def order_geometry_kernel(own_ref, pts_ref, area_ref, out_ref, lhs_ref):
    elems = own_ref.shape[1]

    def read(h):
        at = slice(LOW * h, LOW * h + LOW)
        return jnp.concatenate([pts_ref[:, at], area_ref[:, at] * (1.0 / FOUR_PI)], axis=0)

    stack_parts(read, 3, 4, elems // LOW, lhs_ref)

    def emit(c, total):
        total = total + pltpu.roll(total, 4, 0)
        out_ref[2 * c] = total[:, :CLUSTER]
        out_ref[2 * c + 1] = total[:, CLUSTER:]

    gather_body(own_ref, lhs_ref, 4, 2 * CLUSTER, emit)


def order_geometry(own, points, areas):
    elems = own.shape[1]
    return pl.pallas_call(
        order_geometry_kernel,
        out_shape=jax.ShapeDtypeStruct((elems // CLUSTER, 8, CLUSTER), F32),
        scratch_shapes=[pltpu.VMEM((elems // LOW * 4, 3 * LOW), BF16)],
        name="order_geometry",
    )(outside(own), outside(points), outside(areas))


def return_kernel(own_ref, near_ref, out_ref, lhs_ref, hot_ref, acc_ref):
    width = near_ref.shape[2]
    elems = own_ref.shape[1]
    high_count = elems // LOW
    chunk = lhs_ref.shape[1]
    per = chunk // width
    acc_ref[...] = jnp.zeros_like(acc_ref)

    def step(c, _):
        at = pl.multiple_of(c * chunk, chunk)
        own = own_ref[:, pl.ds(at, chunk)]
        hot_ref[...] = one_hot_low(own & (LOW - 1))
        high = jnp.broadcast_to(own >> 8, (8, chunk))
        for p in range(per):
            lanes = slice(p * width, p * width + width)
            pieces = parts_of(near_ref[c * per + p], 2)
            here = high[:, lanes]
            for h in range(high_count):
                mask = here == h
                both = [jnp.where(mask, piece, 0.0) for piece in pieces]
                lhs_ref[16 * h : 16 * h + 16, lanes] = jnp.concatenate(both, axis=0).astype(BF16)
        acc_ref[...] += lax.dot_general(
            lhs_ref[...], hot_ref[...], (((1,), (1,)), ((), ())), preferred_element_type=F32
        )
        return 0

    lax.fori_loop(0, elems // chunk, step, 0)
    for h in range(high_count):
        out_ref[:, LOW * h : LOW * h + LOW] = (
            acc_ref[16 * h : 16 * h + 8, :] + acc_ref[16 * h + 8 : 16 * h + 16, :]
        )


def return_to_elements(own, values):
    pieces, steps, width = values.shape
    elems = own.shape[1]
    chunk = max(1024, width)
    return pl.pallas_call(
        return_kernel,
        out_shape=jax.ShapeDtypeStruct((steps, elems), F32),
        scratch_shapes=[
            pltpu.VMEM((elems // LOW * 16, chunk), BF16),
            pltpu.VMEM((LOW, chunk), BF16),
            pltpu.VMEM((elems // LOW * 16, LOW), F32),
        ],
        name="return_to_elements",
    )(held(own), held(values))


def forward_kernel(split, table_ref, x_ref, out_ref):
    steps, width = x_ref.shape
    half = width // split
    stacked = jnp.concatenate([x_ref[:, half * s : half * s + half] for s in range(split)], axis=0)
    out_ref[...] = jnp.dot(
        table_ref[...], stacked, precision=lax.Precision.HIGHEST, preferred_element_type=F32
    )


def forward_transform(table, x, split):
    return pl.pallas_call(
        functools.partial(forward_kernel, split),
        out_shape=pltpu.VMEM((table.shape[0], x.shape[1] // split), F32),
        name="forward_transform",
    )(held(table), held(x))


def inverse_kernel(split, table_ref, x_ref, out_ref):
    total, half = x_ref.shape
    dests, steps_local, _ = out_ref.shape
    steps = dests * steps_local
    values = jnp.dot(
        table_ref[...], x_ref[...], precision=lax.Precision.HIGHEST, preferred_element_type=F32
    )
    for s in range(split):
        for d in range(dests):
            at = s * steps + d * steps_local
            out_ref[d, :, half * s : half * s + half] = values[at : at + steps_local]


def inverse_transform(table, x, split, dests):
    steps = table.shape[0] // split
    return pl.pallas_call(
        functools.partial(inverse_kernel, split),
        out_shape=pltpu.VMEM((dests, steps // dests, x.shape[1] * split), F32),
        name="inverse_transform",
    )(held(table), held(x))


def split_points(x):
    n = jnp.round(x * GRID)
    h = n * (1.0 / GRID)
    low = x - h
    norm = jnp.sum(n * n, axis=0, keepdims=True)
    bias = jnp.sum((2.0 * h + low) * low, axis=0, keepdims=True)
    return n, h, parts_of(low, 3), norm, bias


def distance_terms(x):
    n, h, (l1, l2, l3), norm, bias = split_points(x)
    one = jnp.ones_like(bias)
    zero3, zero = jnp.zeros_like(n), jnp.zeros((TERMS - 36, LANES), F32)
    norm = parts_of(norm, 3)
    left = [n, n, n, *norm, one, one, one, l1, l1, l1, l2, l2, l3, *parts_of(bias, 3), zero]
    unit = 1.0 / GRID**2
    flat = one * unit
    exact = [n * (-2.0 * unit), zero3, zero3, flat, flat, flat, *(p * unit for p in norm)]
    exact += [zero3] * 7 + [zero]
    rest = [p * (-2.0 / GRID) for p in (l1, l2, l3)]
    rest += [zero3, *parts_of(bias + SOFTEN * SOFTEN, 3)]
    rest += [p * -2.0 for p in (h, l1, l2, h, l1, h)] + [one, one, one, zero]
    return [jnp.concatenate(rows, axis=0).astype(BF16) for rows in (left, exact, rest)]


def near_kernel(
    cfg,
    coef,
    rows,
    cols,
    live,
    geo_ref,
    val_ref,
    sel_ref,
    out_ref,
    acc_ref,
    col_ref,
    row_ref,
    feat_ref,
    buf_a,
    buf_b,
):
    each, split, groups, group_clusters, cap, own_groups, per_piece, feats = cfg
    my_group = lax.axis_index("elem")
    mine = lax.axis_index("tm")
    if own_groups == groups:
        mine = mine * split + my_group
    clusters = geo_ref.shape[0]
    per_half = per_piece // split
    pieces = group_clusters // per_piece
    acc_ref[...] = jnp.zeros_like(acc_ref)

    def prepare(piece, _):
        for g in range(groups):
            index = piece * groups + g if own_groups == groups else g * pieces + piece
            chunk = val_ref[index]
            re, im = chunk[0:FS], chunk[FS : 2 * FS]
            ax, ay = jnp.abs(re), jnp.abs(im)
            large, small = jnp.maximum(ax, ay), jnp.minimum(ax, ay)
            q = small / jnp.maximum(large, 1e-37)
            turn = q * poly(ARCTAN, q * q)
            turn = jnp.where(ay > ax, 0.25 - turn, turn)
            turn = jnp.where(re < 0, 0.5 - turn, turn)
            turn = jnp.where(im < 0, -turn, turn)
            size = large * jnp.sqrt(1.0 + q * q)
            for w in range(per_piece):
                c = g * group_clusters + piece * per_piece + w
                half, lane = w // per_half, (w % per_half) * LANES
                mine_rows = slice(half * each, half * each + each)
                feature = jnp.concatenate(
                    [
                        turn[mine_rows, lane : lane + LANES],
                        size[mine_rows, lane : lane + LANES] * geo_ref[c][3:4],
                    ],
                    axis=0,
                )
                stacked = jnp.concatenate(
                    parts_of(feature, 3) + [jnp.zeros((feats - 6 * each, LANES), F32)], axis=0
                )
                feat_ref[c] = stacked.astype(BF16)
                left, exact, rest = distance_terms(geo_ref[c][0:3])
                col_ref[c] = left
                row_ref[c, :, :LANES] = exact
                row_ref[c, :, LANES:] = rest
        return 0

    lax.fori_loop(0, pieces, prepare, 0)

    decay = [coef[mine * 2 * each + f] for f in range(each)]
    turns = [coef[mine * 2 * each + each + f] for f in range(each)]
    sel = sel_ref[...].astype(BF16)
    lives = [live[g if own_groups == groups else my_group] for g in range(own_groups)]
    total_live = sum(lives)
    idle = own_groups * group_clusters

    def locate(b):
        slot, inside = jnp.int32(0), b
        for g in range(1, own_groups):
            over = inside >= lives[g - 1]
            moved = jnp.logical_and(over, slot == g - 1)
            inside = jnp.where(moved, inside - lives[g - 1], inside)
            slot = jnp.where(moved, g, slot)
        valid = b < total_live
        slot = jnp.where(valid, slot, 0)
        inside = jnp.where(valid, inside, 0)
        group = slot if own_groups == groups else my_group
        at = group * cap + inside
        row = rows[at]
        target = jnp.where(valid, slot * group_clusters + row, idle)
        return group * group_clusters + row, cols[at], target

    def load(b, buf):
        row, col, _ = locate(b)
        product = lambda a, b: lax.dot_general(
            a, b, (((0,), (0,)), ((), ())), preferred_element_type=F32
        )
        buf[:, : 2 * LANES] = product(col_ref[col], row_ref[row])
        buf[:, 2 * LANES :] = product(feat_ref[col], sel)

    def work(b, buf):
        _, _, target = locate(b)
        sums = [jnp.zeros((8, LANES), F32) for _ in range(3 * each)]
        for j in range(CLUSTER // 8):
            lane = lambda k: buf[8 * j : 8 * j + 8, LANES * k : LANES * k + LANES]
            square = lane(0) + lane(1)
            inv = lax.rsqrt(square)
            dist = square * inv
            for f in range(each):
                weight = jnp.exp2(decay[f] * dist) * (inv * lane(2 + each + f))
                t = lane(2 + f) - turns[f] * dist
                t = t - jnp.round(t)
                u = t * t
                s = t * monic(SIN_QUARTER, u)
                half_sin = s * monic(COS_QUARTER, u)
                half_cos = 1.0 / HALF_COS - s * s
                ws = weight * half_sin
                sums[3 * f] += weight
                sums[3 * f + 1] += ws * half_sin
                sums[3 * f + 2] += ws * half_cos
        for f in range(each):
            whole, squared, mixed = sums[3 * f : 3 * f + 3]
            acc_ref[target, f] += whole - (2.0 * HALF_SIN**2) * squared
            acc_ref[target, each + f] += (2.0 * HALF_SIN * HALF_COS) * mixed

    load(jnp.int32(0), buf_a)
    load(jnp.int32(1), buf_b)

    def pair(i, _):
        for q in range(0, 4, 2):
            work(4 * i + q, buf_a)
            load(4 * i + q + 2, buf_a)
            work(4 * i + q + 1, buf_b)
            load(4 * i + q + 3, buf_b)
        return 0

    lax.fori_loop(0, (total_live + 3) // 4, pair, 0)

    def finish(piece, _):
        for slot in range(own_groups):
            for w in range(per_piece):
                c = slot * group_clusters + piece * per_piece + w
                half, lane = w // per_half, (w % per_half) * LANES
                total = jnp.sum(acc_ref[c], axis=1)
                dest = piece * own_groups + slot
                for part in range(2):
                    first = part * FS + half * each
                    out_ref[dest, first : first + each, lane : lane + LANES] = total[
                        part * each : part * each + each
                    ]
        return 0

    lax.fori_loop(0, pieces, finish, 0)


def near_field(coef, rows, cols, live, geometry, values, split, groups, own_groups):
    each = FS // split
    clusters = geometry.shape[0]
    group_clusters = clusters // groups
    per_piece = values.shape[2] // LANES * split
    feats = -(-6 * each // 16) * 16
    sel = np.zeros((feats, 2 * each, LANES), np.float32)
    for k in range(6 * each):
        sel[k, k % (2 * each)] = 1.0
    sel = sel.reshape(feats, 2 * each * LANES)
    cfg = (
        each,
        split,
        groups,
        group_clusters,
        rows.shape[0] // groups,
        own_groups,
        per_piece,
        feats,
    )
    smem = pl.BlockSpec(memory_space=pltpu.SMEM)
    vmem = pl.BlockSpec(memory_space=pltpu.VMEM)
    dests = own_groups * group_clusters // per_piece
    return pl.pallas_call(
        functools.partial(near_kernel, cfg),
        out_shape=pltpu.VMEM((dests, 2 * FS, per_piece // split * LANES), F32),
        in_specs=[smem] * 4 + [vmem] * 3,
        out_specs=vmem,
        scratch_shapes=[
            pltpu.VMEM((own_groups * group_clusters + 1, 2 * each, 8, LANES), F32),
            pltpu.VMEM((clusters, TERMS, CLUSTER), BF16),
            pltpu.VMEM((clusters, TERMS, 2 * LANES), BF16),
            pltpu.VMEM((clusters, feats, CLUSTER), BF16),
            pltpu.VMEM((CLUSTER, (2 + 2 * each) * LANES), F32),
            pltpu.VMEM((CLUSTER, (2 + 2 * each) * LANES), F32),
        ],
        compiler_params=pltpu.CompilerParams(vmem_limit_bytes=56 * 2**20),
        name="near_field",
    )(outside(coef), outside(rows), outside(cols), outside(live), held(geometry), held(values), held(jnp.asarray(sel)))


def per_device(history, points, areas, ownership, block_rows, block_cols, block_live):
    steps_local, elem_local = history.shape
    tm_count = lax.axis_size("tm")
    groups = lax.axis_size("elem")
    steps = steps_local * tm_count
    freqs = FS * tm_count
    width = elem_local // tm_count
    split = groups if groups == 2 and width % (2 * LANES) == 0 else 1
    each = FS // split
    shared = split == groups
    axes = ("tm", "elem") if shared else "tm"
    forward, inverse = packed_tables(steps, freqs, split)
    lap = laplace_table(freqs, steps).reshape(-1, each)
    coefs = np.concatenate([-lap.real / LOG_HALF, lap.imag / (2.0 * np.pi)], axis=1)
    coef = jnp.asarray(coefs.astype(np.float32).reshape(-1))

    own = ownership.reshape(1, elem_local)
    pieces = order_history(own, history, width)
    by_time = lax.all_to_all(
        pieces.reshape(tm_count * steps_local, width), "tm", split_axis=0, concat_axis=0, tiled=True
    )
    geometry = order_geometry(own, points, areas.reshape(1, elem_local))
    geometry = lax.all_gather(geometry, "elem", axis=0, tiled=True)
    spectra = forward_transform(jnp.asarray(forward), by_time, split)
    slab = lax.all_to_all(spectra, axes, split_axis=0, concat_axis=0, tiled=True)
    if not shared:
        slab = lax.all_gather(slab, "elem", axis=0, tiled=True)
    slab = slab.reshape(-1, 2 * FS, width // split)
    near = near_field(
        coef,
        block_rows,
        block_cols,
        block_live,
        geometry,
        slab,
        split,
        groups,
        groups if shared else 1,
    )
    near = lax.all_to_all(
        near.reshape(-1, width // split), axes, split_axis=0, concat_axis=0, tiled=True
    )
    rows = inverse_transform(jnp.asarray(inverse), near, split, tm_count)
    rows = lax.all_to_all(
        rows.reshape(steps, width), "tm", split_axis=0, concat_axis=0, tiled=True
    )
    return return_to_elements(own, rows.reshape(tm_count, steps_local, width))


def solution(mesh):
    return jax.shard_map(
        per_device,
        mesh=mesh,
        in_specs=(P("tm", "elem"), P(None, "elem"), P("elem"), P("elem"), P(), P(), P()),
        out_specs=P("tm", "elem"),
        check_vma=False,
    )
```

```python
import functools
import math

import jax
import jax.numpy as jnp
import numpy as np
from jax import lax
from jax.experimental import pallas as pl
from jax.experimental.pallas import tpu as pltpu
from jax.sharding import PartitionSpec as P

FS = 4
CLUSTER = 128
LANES = 128
LOG_HALF = 0.6931471805599453
SOFTEN = 0.05
INV_STEP = 4.0
FOUR_PI = 4.0 * math.pi
LOW = 256
GRID = 64
TERMS = 48
UNROLL = 16
RETURN_CHUNK = 4096
F32 = jnp.float32
BF16 = jnp.bfloat16


def fit(func, high, degree):
    nodes = (np.cos((np.arange(600) + 0.5) / 600 * np.pi) + 1) * (high / 2)
    series = np.polynomial.chebyshev.Chebyshev.fit(
        nodes, func(nodes), degree, domain=[0, high]
    )
    return [float(v) for v in series.convert(kind=np.polynomial.Polynomial).coef]


SIN_QUARTER = fit(lambda u: np.sin(np.pi / 2 * np.sqrt(u)) / np.sqrt(u), 0.25, 2)
COS_QUARTER = fit(lambda u: np.cos(np.pi / 2 * np.sqrt(u)), 0.25, 3)
HALF_SIN = 2.0 * SIN_QUARTER[-1] * COS_QUARTER[-1]
HALF_COS = 2.0 * SIN_QUARTER[-1] ** 2
ARCTAN = fit(lambda u: np.arctan(np.sqrt(u)) / np.sqrt(u) / (2 * np.pi), 1.0, 9)


def poly(coefs, u):
    total = jnp.full_like(u, coefs[-1])
    for value in coefs[-2::-1]:
        total = total * u + value
    return total


def monic(coefs, u):
    total = u + coefs[-2] / coefs[-1]
    for value in coefs[-3::-1]:
        total = total * u + value / coefs[-1]
    return total


def transform_tables(steps, freqs):
    time_ids = np.arange(steps)
    levels = np.arange(freqs)
    phase = (levels[:, None] * time_ids[None, :] % steps) * (2.0 * np.pi / steps)
    decay = np.exp2(-time_ids / steps)
    forward = np.stack([np.cos(phase) * decay, -np.sin(phase) * decay])
    weight = np.where(levels == 0, 1.0, 2.0)[:, None] / (decay * steps)[None, :]
    inverse = np.stack([np.cos(phase) * weight, -np.sin(phase) * weight])
    return forward, inverse


def laplace_table(freqs, steps):
    angles = np.arange(freqs) * (2.0 * np.pi / steps)
    zeta = math.exp(-LOG_HALF / steps) * np.exp(1j * angles)
    delta = (1.0 - zeta) + 0.5 * (1.0 - zeta) ** 2
    return INV_STEP * delta


def packed_tables(steps, freqs, split):
    forward, inverse = transform_tables(steps, freqs)
    each = FS // split
    dests = freqs // each
    fwd = np.zeros((dests, 2, split, each, split, steps), np.float64)
    inv = np.zeros((dests, 2, split, each, split, steps), np.float64)
    for half in range(split):
        rows = forward.reshape(2, dests, each, steps).transpose(1, 0, 2, 3)
        fwd[:, :, half, :, half, :] = rows
        rows = inverse.reshape(2, dests, each, steps).transpose(1, 0, 2, 3)
        inv[:, :, half, :, half, :] = rows
    fwd = fwd.reshape(dests * 2 * FS, split * steps)
    inv = inv.reshape(dests * 2 * FS, split * steps).T
    return fwd.astype(np.float32), np.ascontiguousarray(inv).astype(np.float32)


def held(x):
    return pltpu.with_memory_space_constraint(x, pltpu.VMEM)


def outside(x):
    return pltpu.with_memory_space_constraint(x, pltpu.HBM)


def parts_of(x, count):
    out = []
    for _ in range(count - 1):
        head = x.astype(BF16).astype(F32)
        out.append(head)
        x = x - head
    return out + [x]


def one_hot_low(low_row):
    width = low_row.shape[1]
    ids = lax.broadcasted_iota(jnp.int32, (LOW, width), 0)
    return jnp.where(ids == low_row, 1.0, 0.0).astype(BF16)


def stack_parts(read, count, rows, high_count, lhs_ref):
    group = 16 // rows
    for h in range(0, high_count, group):
        pieces = [parts_of(read(h + i), count) for i in range(group)]
        for part in range(count):
            block = jnp.concatenate([piece[part] for piece in pieces], axis=0)
            lhs_ref[h * rows : h * rows + 16, part * LOW : part * LOW + LOW] = block.astype(BF16)


def gather_body(own_ref, lhs_ref, rows, chunk, emit):
    count = lhs_ref.shape[1] // LOW
    each = 8 // rows
    stride = 16 if each == 1 else 8

    def step(c, _):
        at = pl.multiple_of(c * chunk, chunk)
        own = own_ref[:, pl.ds(at, chunk)]
        high = jnp.broadcast_to(own >> 8, (8, chunk))
        if each > 1:
            high = high - lax.broadcasted_iota(jnp.int32, (8, chunk), 0) // rows
        hot = one_hot_low(own & (LOW - 1))
        picked = jnp.dot(
            lhs_ref[...], jnp.concatenate([hot] * count, axis=0), preferred_element_type=F32
        )
        total = jnp.zeros((8, chunk), F32)
        for v in range(picked.shape[0] // stride):
            value = picked[stride * v : stride * v + 8]
            if stride == 16:
                value = value + picked[16 * v + 8 : 16 * v + 16]
            total += jnp.where(high == v * each, value, 0.0)
        emit(c, total)
        return 0

    lax.fori_loop(0, own_ref.shape[1] // chunk, step, 0, unroll=UNROLL)


def order_history_kernel(own_ref, hist_ref, out_ref, lhs_ref):
    elems = own_ref.shape[1]
    width = out_ref.shape[2]
    chunk = min(256, width)
    for h in range(elems // LOW):
        pieces = parts_of(hist_ref[:, LOW * h : LOW * h + LOW], 2)
        lhs_ref[16 * h : 16 * h + 16, :] = jnp.concatenate(pieces, axis=0).astype(BF16)
    per = width // chunk

    def emit(c, total):
        at = pl.multiple_of(lax.rem(c, per) * chunk, chunk)
        out_ref[c // per, :, pl.ds(at, chunk)] = total

    gather_body(own_ref, lhs_ref, 8, chunk, emit)


def order_history(own, history, width):
    steps, elems = history.shape
    return pl.pallas_call(
        order_history_kernel,
        out_shape=pltpu.VMEM((elems // width, steps, width), F32),
        scratch_shapes=[pltpu.VMEM((elems // LOW * 16, LOW), BF16)],
        name="order_history",
    )(outside(own), outside(history))


def order_geometry_kernel(own_ref, pts_ref, area_ref, out_ref, lhs_ref):
    elems = own_ref.shape[1]

    def read(h):
        at = slice(LOW * h, LOW * h + LOW)
        return jnp.concatenate([pts_ref[:, at], area_ref[:, at] * (1.0 / FOUR_PI)], axis=0)

    stack_parts(read, 3, 4, elems // LOW, lhs_ref)

    def emit(c, total):
        total = total + pltpu.roll(total, 4, 0)
        out_ref[2 * c] = total[:, :CLUSTER]
        out_ref[2 * c + 1] = total[:, CLUSTER:]

    gather_body(own_ref, lhs_ref, 4, 2 * CLUSTER, emit)


def order_geometry(own, points, areas):
    elems = own.shape[1]
    return pl.pallas_call(
        order_geometry_kernel,
        out_shape=jax.ShapeDtypeStruct((elems // CLUSTER, 8, CLUSTER), F32),
        scratch_shapes=[pltpu.VMEM((elems // LOW * 4, 3 * LOW), BF16)],
        name="order_geometry",
    )(outside(own), outside(points), outside(areas))


def return_kernel(own_ref, near_ref, out_ref, lhs_a, lhs_b, hot_a, hot_b, acc_ref):
    width = near_ref.shape[2]
    elems = own_ref.shape[1]
    high_count = elems // LOW
    chunk = lhs_a.shape[1]
    per = chunk // width
    acc_ref[...] = jnp.zeros_like(acc_ref)

    def scattered(c, lhs_ref, hot_ref):
        at = pl.multiple_of(c * chunk, chunk)
        own = own_ref[:, pl.ds(at, chunk)]
        hot_ref[...] = one_hot_low(own & (LOW - 1))
        high = jnp.broadcast_to(own >> 8, (8, chunk))
        for p in range(per):
            lanes = slice(p * width, p * width + width)
            pieces = parts_of(near_ref[c * per + p], 2)
            here = high[:, lanes]
            for h in range(high_count):
                mask = here == h
                both = [jnp.where(mask, piece, 0.0) for piece in pieces]
                lhs_ref[16 * h : 16 * h + 16, lanes] = jnp.concatenate(both, axis=0).astype(BF16)
        return lax.dot_general(
            lhs_ref[...], hot_ref[...], (((1,), (1,)), ((), ())), preferred_element_type=F32
        )

    def step(i, _):
        one = scattered(2 * i, lhs_a, hot_a)
        acc_ref[...] += one + scattered(2 * i + 1, lhs_b, hot_b)
        return 0

    lax.fori_loop(0, elems // (2 * chunk), step, 0)
    for h in range(high_count):
        out_ref[:, LOW * h : LOW * h + LOW] = (
            acc_ref[16 * h : 16 * h + 8, :] + acc_ref[16 * h + 8 : 16 * h + 16, :]
        )


def return_to_elements(own, values):
    pieces, steps, width = values.shape
    elems = own.shape[1]
    chunk = max(RETURN_CHUNK, width)
    return pl.pallas_call(
        return_kernel,
        out_shape=jax.ShapeDtypeStruct((steps, elems), F32),
        scratch_shapes=[pltpu.VMEM((elems // LOW * 16, chunk), BF16)] * 2
        + [pltpu.VMEM((LOW, chunk), BF16)] * 2
        + [pltpu.VMEM((elems // LOW * 16, LOW), F32)],
        name="return_to_elements",
    )(held(own), held(values))


def forward_kernel(split, table_ref, x_ref, out_ref):
    steps, width = x_ref.shape
    half = width // split
    stacked = jnp.concatenate([x_ref[:, half * s : half * s + half] for s in range(split)], axis=0)
    out_ref[...] = jnp.dot(
        table_ref[...], stacked, precision=lax.Precision.HIGHEST, preferred_element_type=F32
    )


def forward_transform(table, x, split):
    return pl.pallas_call(
        functools.partial(forward_kernel, split),
        out_shape=pltpu.VMEM((table.shape[0], x.shape[1] // split), F32),
        name="forward_transform",
    )(held(table), held(x))


def inverse_kernel(split, table_ref, x_ref, out_ref):
    total, half = x_ref.shape
    dests, steps_local, _ = out_ref.shape
    steps = dests * steps_local
    values = jnp.dot(
        table_ref[...], x_ref[...], precision=lax.Precision.HIGHEST, preferred_element_type=F32
    )
    for s in range(split):
        for d in range(dests):
            at = s * steps + d * steps_local
            out_ref[d, :, half * s : half * s + half] = values[at : at + steps_local]


def inverse_transform(table, x, split, dests):
    steps = table.shape[0] // split
    return pl.pallas_call(
        functools.partial(inverse_kernel, split),
        out_shape=pltpu.VMEM((dests, steps // dests, x.shape[1] * split), F32),
        name="inverse_transform",
    )(held(table), held(x))


def distance_terms(x):
    row = lax.broadcasted_iota(jnp.int32, x.shape, 0)
    first = row < 4
    third, seventh = row == 3, row == 7
    either = jnp.logical_or(third, seventh)
    zero, one = jnp.zeros_like(x), jnp.ones_like(x)

    def over_coords(v):
        v = jnp.where(either, 0.0, v)
        return v + pltpu.roll(v, 1, 0) + pltpu.roll(v, 2, 0) + pltpu.roll(v, 3, 0)

    def rows(top, bottom, three, seven):
        value = top if top is bottom else jnp.where(first, top, bottom)
        if three is seven:
            return jnp.where(either, three, value)
        return jnp.where(third, three, jnp.where(seventh, seven, value))

    def joined(*blocks):
        return jnp.concatenate([*blocks, zero], axis=0).astype(BF16)

    n = jnp.round(x * GRID)
    h = n * (1.0 / GRID)
    low = x - h
    l1, l2, l3 = parts_of(low, 3)
    n1, n2, n3 = parts_of(over_coords(n * n), 3)
    bias = over_coords((2.0 * h + low) * low)
    b1, b2, b3 = parts_of(bias, 3)
    left = joined(
        rows(n, n, n1, n2),
        rows(n, l1, n3, one),
        rows(l1, l1, one, one),
        rows(l2, l2, b1, b2),
        rows(l3, zero, b3, zero),
    )
    unit = 1.0 / GRID**2
    flat = one * unit
    exact = joined(
        rows(n * (-2.0 * unit), zero, flat, flat),
        rows(zero, zero, flat, n1 * unit),
        rows(zero, zero, n2 * unit, n3 * unit),
        zero,
        zero,
    )
    b1, b2, b3 = parts_of(bias + SOFTEN * SOFTEN, 3)
    g1, g2, g3 = (p * (-2.0 / GRID) for p in (l1, l2, l3))
    d1, d2, dh = (p * -2.0 for p in (l1, l2, h))
    rest = joined(
        rows(g1, g2, zero, zero),
        rows(g3, dh, zero, b1),
        rows(d1, d2, b2, b3),
        rows(dh, d1, one, one),
        rows(dh, zero, one, zero),
    )
    return left, exact, rest


def near_kernel(
    cfg,
    coef,
    rows,
    cols,
    live,
    geo_ref,
    val_ref,
    sel_ref,
    out_ref,
    acc_ref,
    col_ref,
    row_ref,
    feat_ref,
    buf_a,
    buf_b,
):
    each, split, groups, group_clusters, cap, own_groups, per_piece, feats = cfg
    my_group = lax.axis_index("elem")
    mine = lax.axis_index("tm")
    if own_groups == groups:
        mine = mine * split + my_group
    clusters = geo_ref.shape[0]
    per_half = per_piece // split
    pieces = group_clusters // per_piece
    acc_ref[...] = jnp.zeros_like(acc_ref)

    is_size = lax.broadcasted_iota(jnp.int32, (2 * FS, LANES), 0) >= FS

    def prepare(piece, _):
        for g in range(groups):
            index = piece * groups + g if own_groups == groups else g * pieces + piece
            chunk = val_ref[index]
            re, im = chunk[0:FS], chunk[FS : 2 * FS]
            ax, ay = jnp.abs(re), jnp.abs(im)
            large, small = jnp.maximum(ax, ay), jnp.minimum(ax, ay)
            q = small / jnp.maximum(large, 1e-37)
            turn = q * poly(ARCTAN, q * q)
            turn = jnp.where(ay > ax, 0.25 - turn, turn)
            turn = jnp.where(re < 0, 0.5 - turn, turn)
            turn = jnp.where(im < 0, -turn, turn)
            size = large * jnp.sqrt(1.0 + q * q)
            both = jnp.concatenate([turn, size], axis=0)
            for w in range(per_piece):
                c = g * group_clusters + piece * per_piece + w
                half, lane = w // per_half, (w % per_half) * LANES
                place = geo_ref[c]
                scale = jnp.where(is_size, place[3:4], 1.0)
                feature = both[:, lane : lane + LANES] * scale
                if half:
                    feature = pltpu.roll(feature, 2 * FS - half * each, 0)
                feat_ref[c] = jnp.concatenate(
                    [*parts_of(feature, 3), jnp.zeros_like(feature)], axis=0
                ).astype(BF16)
                left, exact, rest = distance_terms(place)
                col_ref[c] = left
                row_ref[c, :, :LANES] = exact
                row_ref[c, :, LANES:] = rest
        return 0

    lax.fori_loop(0, pieces, prepare, 0)

    decay = [coef[mine * 2 * each + f] for f in range(each)]
    turns = [coef[mine * 2 * each + each + f] for f in range(each)]
    sel = sel_ref[...].astype(BF16)
    lives = [live[g if own_groups == groups else my_group] for g in range(own_groups)]
    total_live = sum(lives)
    idle = own_groups * group_clusters

    def locate(b):
        slot, inside = jnp.int32(0), b
        for g in range(1, own_groups):
            over = inside >= lives[g - 1]
            moved = jnp.logical_and(over, slot == g - 1)
            inside = jnp.where(moved, inside - lives[g - 1], inside)
            slot = jnp.where(moved, g, slot)
        valid = b < total_live
        slot = jnp.where(valid, slot, 0)
        inside = jnp.where(valid, inside, 0)
        group = slot if own_groups == groups else my_group
        at = group * cap + inside
        row = rows[at]
        target = jnp.where(valid, slot * group_clusters + row, idle)
        return group * group_clusters + row, cols[at], target

    def load(b, buf):
        row, col, _ = locate(b)
        product = lambda a, b: lax.dot_general(
            a, b, (((0,), (0,)), ((), ())), preferred_element_type=F32
        )
        buf[:, : 2 * LANES] = product(col_ref[col], row_ref[row])
        buf[:, 2 * LANES :] = product(feat_ref[col], sel)

    def work(b, buf):
        _, _, target = locate(b)
        sums = [jnp.zeros((8, LANES), F32) for _ in range(3 * each)]
        for j in range(CLUSTER // 8):
            lane = lambda k: buf[8 * j : 8 * j + 8, LANES * k : LANES * k + LANES]
            square = lane(0) + lane(1)
            inv = lax.rsqrt(square)
            dist = square * inv
            for f in range(each):
                weight = jnp.exp2(decay[f] * dist) * (inv * lane(2 + each + f))
                t = lane(2 + f) - turns[f] * dist
                t = t - jnp.round(t)
                u = t * t
                s = t * monic(SIN_QUARTER, u)
                half_sin = s * monic(COS_QUARTER, u)
                half_cos = 1.0 / HALF_COS - s * s
                ws = weight * half_sin
                sums[3 * f] += weight
                sums[3 * f + 1] += ws * half_sin
                sums[3 * f + 2] += ws * half_cos
        for f in range(each):
            whole, squared, mixed = sums[3 * f : 3 * f + 3]
            acc_ref[target, f] += whole - (2.0 * HALF_SIN**2) * squared
            acc_ref[target, each + f] += (2.0 * HALF_SIN * HALF_COS) * mixed

    load(jnp.int32(0), buf_a)
    load(jnp.int32(1), buf_b)

    def pair(i, _):
        for q in range(0, 4, 2):
            work(4 * i + q, buf_a)
            load(4 * i + q + 2, buf_a)
            work(4 * i + q + 1, buf_b)
            load(4 * i + q + 3, buf_b)
        return 0

    lax.fori_loop(0, (total_live + 3) // 4, pair, 0)

    def finish(piece, _):
        for slot in range(own_groups):
            for w in range(per_piece):
                c = slot * group_clusters + piece * per_piece + w
                half, lane = w // per_half, (w % per_half) * LANES
                total = jnp.sum(acc_ref[c], axis=1)
                dest = piece * own_groups + slot
                for part in range(2):
                    first = part * FS + half * each
                    out_ref[dest, first : first + each, lane : lane + LANES] = total[
                        part * each : part * each + each
                    ]
        return 0

    lax.fori_loop(0, pieces, finish, 0)


def near_field(coef, rows, cols, live, geometry, values, split, groups, own_groups):
    each = FS // split
    clusters = geometry.shape[0]
    group_clusters = clusters // groups
    per_piece = values.shape[2] // LANES * split
    feats = 8 * FS
    sel = np.zeros((feats, 2 * each, LANES), np.float32)
    for part in range(3):
        for f in range(each):
            sel[part * 2 * FS + f, f] = 1.0
            sel[part * 2 * FS + FS + f, each + f] = 1.0
    sel = sel.reshape(feats, 2 * each * LANES)
    cfg = (
        each,
        split,
        groups,
        group_clusters,
        rows.shape[0] // groups,
        own_groups,
        per_piece,
        feats,
    )
    smem = pl.BlockSpec(memory_space=pltpu.SMEM)
    vmem = pl.BlockSpec(memory_space=pltpu.VMEM)
    dests = own_groups * group_clusters // per_piece
    return pl.pallas_call(
        functools.partial(near_kernel, cfg),
        out_shape=pltpu.VMEM((dests, 2 * FS, per_piece // split * LANES), F32),
        in_specs=[smem] * 4 + [vmem] * 3,
        out_specs=vmem,
        scratch_shapes=[
            pltpu.VMEM((own_groups * group_clusters + 1, 2 * each, 8, LANES), F32),
            pltpu.VMEM((clusters, TERMS, CLUSTER), BF16),
            pltpu.VMEM((clusters, TERMS, 2 * LANES), BF16),
            pltpu.VMEM((clusters, feats, CLUSTER), BF16),
            pltpu.VMEM((CLUSTER, (2 + 2 * each) * LANES), F32),
            pltpu.VMEM((CLUSTER, (2 + 2 * each) * LANES), F32),
        ],
        compiler_params=pltpu.CompilerParams(vmem_limit_bytes=56 * 2**20),
        name="near_field",
    )(outside(coef), outside(rows), outside(cols), outside(live), held(geometry), held(values), held(jnp.asarray(sel)))


def per_device(history, points, areas, ownership, block_rows, block_cols, block_live):
    steps_local, elem_local = history.shape
    tm_count = lax.axis_size("tm")
    groups = lax.axis_size("elem")
    steps = steps_local * tm_count
    freqs = FS * tm_count
    width = elem_local // tm_count
    split = groups if groups == 2 and width % (2 * LANES) == 0 else 1
    each = FS // split
    shared = split == groups
    axes = ("tm", "elem") if shared else "tm"
    forward, inverse = packed_tables(steps, freqs, split)
    lap = laplace_table(freqs, steps).reshape(-1, each)
    coefs = np.concatenate([-lap.real / LOG_HALF, lap.imag / (2.0 * np.pi)], axis=1)
    coef = jnp.asarray(coefs.astype(np.float32).reshape(-1))

    own = ownership.reshape(1, elem_local)
    pieces = order_history(own, history, width)
    by_time = lax.all_to_all(
        pieces.reshape(tm_count * steps_local, width), "tm", split_axis=0, concat_axis=0, tiled=True
    )
    geometry = order_geometry(own, points, areas.reshape(1, elem_local))
    geometry = lax.all_gather(geometry, "elem", axis=0, tiled=True)
    spectra = forward_transform(jnp.asarray(forward), by_time, split)
    slab = lax.all_to_all(spectra, axes, split_axis=0, concat_axis=0, tiled=True)
    if not shared:
        slab = lax.all_gather(slab, "elem", axis=0, tiled=True)
    slab = slab.reshape(-1, 2 * FS, width // split)
    near = near_field(
        coef,
        block_rows,
        block_cols,
        block_live,
        geometry,
        slab,
        split,
        groups,
        groups if shared else 1,
    )
    near = lax.all_to_all(
        near.reshape(-1, width // split), axes, split_axis=0, concat_axis=0, tiled=True
    )
    rows = inverse_transform(jnp.asarray(inverse), near, split, tm_count)
    rows = lax.all_to_all(
        rows.reshape(steps, width), "tm", split_axis=0, concat_axis=0, tiled=True
    )
    return return_to_elements(own, rows.reshape(tm_count, steps_local, width))


def solution(mesh):
    return jax.shard_map(
        per_device,
        mesh=mesh,
        in_specs=(P("tm", "elem"), P(None, "elem"), P("elem"), P("elem"), P(), P(), P()),
        out_specs=P("tm", "elem"),
        check_vma=False,
    )
```

```python
import functools
import math

import jax
import jax.numpy as jnp
import numpy as np
from jax import lax
from jax.experimental import pallas as pl
from jax.experimental.pallas import tpu as pltpu
from jax.sharding import PartitionSpec as P

FS = 4
CLUSTER = 128
LANES = 128
LOG_HALF = 0.6931471805599453
SOFTEN = 0.05
INV_STEP = 4.0
FOUR_PI = 4.0 * math.pi
LOW = 256
GRID = 64
TERMS = 48
UNROLL = 16
RETURN_CHUNK = 4096
F32 = jnp.float32
BF16 = jnp.bfloat16


def fit(func, high, degree):
    nodes = (np.cos((np.arange(600) + 0.5) / 600 * np.pi) + 1) * (high / 2)
    series = np.polynomial.chebyshev.Chebyshev.fit(
        nodes, func(nodes), degree, domain=[0, high]
    )
    return [float(v) for v in series.convert(kind=np.polynomial.Polynomial).coef]


SIN_QUARTER = fit(lambda u: np.sin(np.pi / 2 * np.sqrt(u)) / np.sqrt(u), 0.25, 2)
COS_QUARTER = fit(lambda u: np.cos(np.pi / 2 * np.sqrt(u)), 0.25, 3)
HALF_SIN = 2.0 * SIN_QUARTER[-1] * COS_QUARTER[-1]
HALF_COS = 2.0 * SIN_QUARTER[-1] ** 2
ARCTAN = fit(lambda u: np.arctan(np.sqrt(u)) / np.sqrt(u) / (2 * np.pi), 1.0, 9)


def poly(coefs, u):
    total = jnp.full_like(u, coefs[-1])
    for value in coefs[-2::-1]:
        total = total * u + value
    return total


def monic(coefs, u):
    total = u + coefs[-2] / coefs[-1]
    for value in coefs[-3::-1]:
        total = total * u + value / coefs[-1]
    return total


def transform_tables(steps, freqs):
    time_ids = np.arange(steps)
    levels = np.arange(freqs)
    phase = (levels[:, None] * time_ids[None, :] % steps) * (2.0 * np.pi / steps)
    decay = np.exp2(-time_ids / steps)
    forward = np.stack([np.cos(phase) * decay, -np.sin(phase) * decay])
    weight = np.where(levels == 0, 1.0, 2.0)[:, None] / (decay * steps)[None, :]
    inverse = np.stack([np.cos(phase) * weight, -np.sin(phase) * weight])
    return forward, inverse


def laplace_table(freqs, steps):
    angles = np.arange(freqs) * (2.0 * np.pi / steps)
    zeta = math.exp(-LOG_HALF / steps) * np.exp(1j * angles)
    delta = (1.0 - zeta) + 0.5 * (1.0 - zeta) ** 2
    return INV_STEP * delta


def packed_tables(steps, freqs, split):
    forward, inverse = transform_tables(steps, freqs)
    each = FS // split
    dests = freqs // each
    fwd = np.zeros((dests, 2, split, each, split, steps), np.float64)
    inv = np.zeros((dests, 2, split, each, split, steps), np.float64)
    for half in range(split):
        rows = forward.reshape(2, dests, each, steps).transpose(1, 0, 2, 3)
        fwd[:, :, half, :, half, :] = rows
        rows = inverse.reshape(2, dests, each, steps).transpose(1, 0, 2, 3)
        inv[:, :, half, :, half, :] = rows
    fwd = fwd.reshape(dests * 2 * FS, split * steps)
    inv = inv.reshape(dests * 2 * FS, split * steps).T
    return fwd.astype(np.float32), np.ascontiguousarray(inv).astype(np.float32)


def held(x):
    return pltpu.with_memory_space_constraint(x, pltpu.VMEM)


def outside(x):
    return pltpu.with_memory_space_constraint(x, pltpu.HBM)


def parts_of(x, count):
    out = []
    for _ in range(count - 1):
        head = x.astype(BF16).astype(F32)
        out.append(head)
        x = x - head
    return out + [x]


def one_hot_low(low_row):
    width = low_row.shape[1]
    ids = lax.broadcasted_iota(jnp.int32, (LOW, width), 0)
    return jnp.where(ids == low_row, 1.0, 0.0).astype(BF16)


def stack_parts(read, count, rows, high_count, lhs_ref):
    group = 16 // rows
    for h in range(0, high_count, group):
        pieces = [parts_of(read(h + i), count) for i in range(group)]
        for part in range(count):
            block = jnp.concatenate([piece[part] for piece in pieces], axis=0)
            lhs_ref[h * rows : h * rows + 16, part * LOW : part * LOW + LOW] = block.astype(BF16)


def gather_body(own_ref, lhs_ref, rows, chunk, emit):
    count = lhs_ref.shape[1] // LOW
    each = 8 // rows
    stride = 16 if each == 1 else 8

    def step(c, _):
        at = pl.multiple_of(c * chunk, chunk)
        own = own_ref[:, pl.ds(at, chunk)]
        high = jnp.broadcast_to(own >> 8, (8, chunk))
        if each > 1:
            high = high - lax.broadcasted_iota(jnp.int32, (8, chunk), 0) // rows
        hot = one_hot_low(own & (LOW - 1))
        picked = jnp.dot(
            lhs_ref[...], jnp.concatenate([hot] * count, axis=0), preferred_element_type=F32
        )
        total = jnp.zeros((8, chunk), F32)
        for v in range(picked.shape[0] // stride):
            value = picked[stride * v : stride * v + 8]
            if stride == 16:
                value = value + picked[16 * v + 8 : 16 * v + 16]
            total += jnp.where(high == v * each, value, 0.0)
        emit(c, total)
        return 0

    lax.fori_loop(0, own_ref.shape[1] // chunk, step, 0, unroll=UNROLL)


def order_history_kernel(own_ref, hist_ref, out_ref, lhs_ref):
    elems = own_ref.shape[1]
    width = out_ref.shape[2]
    chunk = min(256, width)
    for h in range(elems // LOW):
        pieces = parts_of(hist_ref[:, LOW * h : LOW * h + LOW], 2)
        lhs_ref[16 * h : 16 * h + 16, :] = jnp.concatenate(pieces, axis=0).astype(BF16)
    per = width // chunk

    def emit(c, total):
        at = pl.multiple_of(lax.rem(c, per) * chunk, chunk)
        out_ref[c // per, :, pl.ds(at, chunk)] = total

    gather_body(own_ref, lhs_ref, 8, chunk, emit)


def order_history(own, history, width):
    steps, elems = history.shape
    return pl.pallas_call(
        order_history_kernel,
        out_shape=pltpu.VMEM((elems // width, steps, width), F32),
        scratch_shapes=[pltpu.VMEM((elems // LOW * 16, LOW), BF16)],
        name="order_history",
    )(outside(own), outside(history))


def order_geometry_kernel(own_ref, pts_ref, area_ref, out_ref, lhs_ref):
    elems = own_ref.shape[1]

    def read(h):
        at = slice(LOW * h, LOW * h + LOW)
        return jnp.concatenate([pts_ref[:, at], area_ref[:, at] * (1.0 / FOUR_PI)], axis=0)

    stack_parts(read, 3, 4, elems // LOW, lhs_ref)

    def emit(c, total):
        total = total + pltpu.roll(total, 4, 0)
        out_ref[2 * c] = total[:, :CLUSTER]
        out_ref[2 * c + 1] = total[:, CLUSTER:]

    gather_body(own_ref, lhs_ref, 4, 2 * CLUSTER, emit)


def order_geometry(own, points, areas):
    elems = own.shape[1]
    return pl.pallas_call(
        order_geometry_kernel,
        out_shape=jax.ShapeDtypeStruct((elems // CLUSTER, 8, CLUSTER), F32),
        scratch_shapes=[pltpu.VMEM((elems // LOW * 4, 3 * LOW), BF16)],
        name="order_geometry",
    )(outside(own), outside(points), outside(areas))


def return_kernel(own_ref, near_ref, out_ref, lhs_a, lhs_b, hot_a, hot_b, acc_ref):
    width = near_ref.shape[2]
    elems = own_ref.shape[1]
    high_count = elems // LOW
    chunk = lhs_a.shape[1]
    per = chunk // width
    acc_ref[...] = jnp.zeros_like(acc_ref)

    def scattered(c, lhs_ref, hot_ref):
        at = pl.multiple_of(c * chunk, chunk)
        own = own_ref[:, pl.ds(at, chunk)]
        hot_ref[...] = one_hot_low(own & (LOW - 1))
        high = jnp.broadcast_to(own >> 8, (8, chunk))
        for p in range(per):
            lanes = slice(p * width, p * width + width)
            pieces = parts_of(near_ref[c * per + p], 2)
            here = high[:, lanes]
            for h in range(high_count):
                mask = here == h
                both = [jnp.where(mask, piece, 0.0) for piece in pieces]
                lhs_ref[16 * h : 16 * h + 16, lanes] = jnp.concatenate(both, axis=0).astype(BF16)
        return lax.dot_general(
            lhs_ref[...], hot_ref[...], (((1,), (1,)), ((), ())), preferred_element_type=F32
        )

    def step(i, _):
        one = scattered(2 * i, lhs_a, hot_a)
        acc_ref[...] += one + scattered(2 * i + 1, lhs_b, hot_b)
        return 0

    lax.fori_loop(0, elems // (2 * chunk), step, 0)
    for h in range(high_count):
        out_ref[:, LOW * h : LOW * h + LOW] = (
            acc_ref[16 * h : 16 * h + 8, :] + acc_ref[16 * h + 8 : 16 * h + 16, :]
        )


def return_to_elements(own, values):
    pieces, steps, width = values.shape
    elems = own.shape[1]
    chunk = max(RETURN_CHUNK, width)
    return pl.pallas_call(
        return_kernel,
        out_shape=jax.ShapeDtypeStruct((steps, elems), F32),
        scratch_shapes=[pltpu.VMEM((elems // LOW * 16, chunk), BF16)] * 2
        + [pltpu.VMEM((LOW, chunk), BF16)] * 2
        + [pltpu.VMEM((elems // LOW * 16, LOW), F32)],
        name="return_to_elements",
    )(held(own), held(values))


def forward_kernel(split, table_ref, x_ref, out_ref):
    steps, width = x_ref.shape
    half = width // split
    stacked = jnp.concatenate([x_ref[:, half * s : half * s + half] for s in range(split)], axis=0)
    out_ref[...] = jnp.dot(
        table_ref[...], stacked, precision=lax.Precision.HIGHEST, preferred_element_type=F32
    )


def forward_transform(table, x, split):
    return pl.pallas_call(
        functools.partial(forward_kernel, split),
        out_shape=pltpu.VMEM((table.shape[0], x.shape[1] // split), F32),
        name="forward_transform",
    )(held(table), held(x))


def inverse_kernel(split, table_ref, x_ref, out_ref):
    total, half = x_ref.shape
    dests, steps_local, _ = out_ref.shape
    steps = dests * steps_local
    values = jnp.dot(
        table_ref[...], x_ref[...], precision=lax.Precision.HIGHEST, preferred_element_type=F32
    )
    for s in range(split):
        for d in range(dests):
            at = s * steps + d * steps_local
            out_ref[d, :, half * s : half * s + half] = values[at : at + steps_local]


def inverse_transform(table, x, split, dests):
    steps = table.shape[0] // split
    return pl.pallas_call(
        functools.partial(inverse_kernel, split),
        out_shape=pltpu.VMEM((dests, steps // dests, x.shape[1] * split), F32),
        name="inverse_transform",
    )(held(table), held(x))


def distance_terms(x):
    row = lax.broadcasted_iota(jnp.int32, x.shape, 0)
    first = row < 4
    third, seventh = row == 3, row == 7
    either = jnp.logical_or(third, seventh)
    zero, one = jnp.zeros_like(x), jnp.ones_like(x)

    def over_coords(v):
        v = jnp.where(either, 0.0, v)
        return v + pltpu.roll(v, 1, 0) + pltpu.roll(v, 2, 0) + pltpu.roll(v, 3, 0)

    def rows(top, bottom, three, seven):
        value = top if top is bottom else jnp.where(first, top, bottom)
        if three is seven:
            return jnp.where(either, three, value)
        return jnp.where(third, three, jnp.where(seventh, seven, value))

    def joined(*blocks):
        return jnp.concatenate([*blocks, zero], axis=0).astype(BF16)

    n = jnp.round(x * GRID)
    h = n * (1.0 / GRID)
    low = x - h
    l1, l2, l3 = parts_of(low, 3)
    n1, n2, n3 = parts_of(over_coords(n * n), 3)
    bias = over_coords((2.0 * h + low) * low)
    b1, b2, b3 = parts_of(bias, 3)
    left = joined(
        rows(n, n, n1, n2),
        rows(n, l1, n3, one),
        rows(l1, l1, one, one),
        rows(l2, l2, b1, b2),
        rows(l3, zero, b3, zero),
    )
    unit = 1.0 / GRID**2
    flat = one * unit
    exact = joined(
        rows(n * (-2.0 * unit), zero, flat, flat),
        rows(zero, zero, flat, n1 * unit),
        rows(zero, zero, n2 * unit, n3 * unit),
        zero,
        zero,
    )
    b1, b2, b3 = parts_of(bias + SOFTEN * SOFTEN, 3)
    g1, g2, g3 = (p * (-2.0 / GRID) for p in (l1, l2, l3))
    d1, d2, dh = (p * -2.0 for p in (l1, l2, h))
    rest = joined(
        rows(g1, g2, zero, zero),
        rows(g3, dh, zero, b1),
        rows(d1, d2, b2, b3),
        rows(dh, d1, one, one),
        rows(dh, zero, one, zero),
    )
    return left, exact, rest


def near_kernel(
    cfg,
    coef,
    rows,
    cols,
    live,
    geo_ref,
    val_ref,
    sel_ref,
    out_ref,
    acc_ref,
    col_ref,
    row_ref,
    feat_ref,
    buf_a,
    buf_b,
):
    each, split, groups, group_clusters, cap, own_groups, per_piece, feats = cfg
    my_group = lax.axis_index("elem")
    mine = lax.axis_index("tm")
    if own_groups == groups:
        mine = mine * split + my_group
    clusters = geo_ref.shape[0]
    per_half = per_piece // split
    pieces = group_clusters // per_piece
    acc_ref[...] = jnp.zeros_like(acc_ref)

    is_size = lax.broadcasted_iota(jnp.int32, (2 * FS, LANES), 0) >= FS

    def prepare(piece, _):
        for g in range(groups):
            index = piece * groups + g if own_groups == groups else g * pieces + piece
            chunk = val_ref[index]
            re, im = chunk[0:FS], chunk[FS : 2 * FS]
            ax, ay = jnp.abs(re), jnp.abs(im)
            large, small = jnp.maximum(ax, ay), jnp.minimum(ax, ay)
            q = small / jnp.maximum(large, 1e-37)
            turn = q * poly(ARCTAN, q * q)
            turn = jnp.where(ay > ax, 0.25 - turn, turn)
            turn = jnp.where(re < 0, 0.5 - turn, turn)
            turn = jnp.where(im < 0, -turn, turn)
            size = large * jnp.sqrt(1.0 + q * q)
            both = jnp.concatenate([turn, size], axis=0)
            for w in range(per_piece):
                c = g * group_clusters + piece * per_piece + w
                half, lane = w // per_half, (w % per_half) * LANES
                place = geo_ref[c]
                scale = jnp.where(is_size, place[3:4], 1.0)
                feature = both[:, lane : lane + LANES] * scale
                if half:
                    feature = pltpu.roll(feature, 2 * FS - half * each, 0)
                feat_ref[c] = jnp.concatenate(
                    [*parts_of(feature, 3), jnp.zeros_like(feature)], axis=0
                ).astype(BF16)
                left, exact, rest = distance_terms(place)
                col_ref[c] = left
                row_ref[c, :, :LANES] = exact
                row_ref[c, :, LANES:] = rest
        return 0

    lax.fori_loop(0, pieces, prepare, 0)

    decay = [coef[mine * 2 * each + f] for f in range(each)]
    turns = [coef[mine * 2 * each + each + f] for f in range(each)]
    sel = sel_ref[...].astype(BF16)
    lives = [live[g if own_groups == groups else my_group] for g in range(own_groups)]
    total_live = sum(lives)
    idle = own_groups * group_clusters

    def locate(b):
        slot, inside = jnp.int32(0), b
        for g in range(1, own_groups):
            over = inside >= lives[g - 1]
            moved = jnp.logical_and(over, slot == g - 1)
            inside = jnp.where(moved, inside - lives[g - 1], inside)
            slot = jnp.where(moved, g, slot)
        valid = b < total_live
        slot = jnp.where(valid, slot, 0)
        inside = jnp.where(valid, inside, 0)
        group = slot if own_groups == groups else my_group
        at = group * cap + inside
        row = rows[at]
        target = jnp.where(valid, slot * group_clusters + row, idle)
        return group * group_clusters + row, cols[at], target

    def load(b, buf):
        row, col, _ = locate(b)
        product = lambda a, b: lax.dot_general(
            a, b, (((0,), (0,)), ((), ())), preferred_element_type=F32
        )
        buf[:, : 2 * LANES] = product(col_ref[col], row_ref[row])
        buf[:, 2 * LANES :] = product(feat_ref[col], sel)

    def work(b, buf):
        _, _, target = locate(b)
        sums = [jnp.zeros((8, LANES), F32) for _ in range(3 * each)]
        for j in range(CLUSTER // 8):
            lane = lambda k: buf[8 * j : 8 * j + 8, LANES * k : LANES * k + LANES]
            square = lane(0) + lane(1)
            inv = lax.rsqrt(square)
            dist = square * inv
            for f in range(each):
                weight = jnp.exp2(decay[f] * dist) * (inv * lane(2 + each + f))
                t = lane(2 + f) - turns[f] * dist
                t = t - jnp.round(t)
                u = t * t
                s = t * monic(SIN_QUARTER, u)
                half_sin = s * monic(COS_QUARTER, u)
                half_cos = 1.0 / HALF_COS - s * s
                ws = weight * half_sin
                sums[3 * f] += weight
                sums[3 * f + 1] += ws * half_sin
                sums[3 * f + 2] += ws * half_cos
        for f in range(each):
            whole, squared, mixed = sums[3 * f : 3 * f + 3]
            acc_ref[target, f] += whole - (2.0 * HALF_SIN**2) * squared
            acc_ref[target, each + f] += (2.0 * HALF_SIN * HALF_COS) * mixed

    load(jnp.int32(0), buf_a)
    load(jnp.int32(1), buf_b)

    def pair(i, _):
        for q in range(0, 6, 2):
            work(6 * i + q, buf_a)
            load(6 * i + q + 2, buf_a)
            work(6 * i + q + 1, buf_b)
            load(6 * i + q + 3, buf_b)
        return 0

    lax.fori_loop(0, (total_live + 5) // 6, pair, 0)

    def finish(piece, _):
        for slot in range(own_groups):
            for w in range(per_piece):
                c = slot * group_clusters + piece * per_piece + w
                half, lane = w // per_half, (w % per_half) * LANES
                total = jnp.sum(acc_ref[c], axis=1)
                dest = piece * own_groups + slot
                for part in range(2):
                    first = part * FS + half * each
                    out_ref[dest, first : first + each, lane : lane + LANES] = total[
                        part * each : part * each + each
                    ]
        return 0

    lax.fori_loop(0, pieces, finish, 0)


def near_field(coef, rows, cols, live, geometry, values, split, groups, own_groups):
    each = FS // split
    clusters = geometry.shape[0]
    group_clusters = clusters // groups
    per_piece = values.shape[2] // LANES * split
    feats = 8 * FS
    sel = np.zeros((feats, 2 * each, LANES), np.float32)
    for part in range(3):
        for f in range(each):
            sel[part * 2 * FS + f, f] = 1.0
            sel[part * 2 * FS + FS + f, each + f] = 1.0
    sel = sel.reshape(feats, 2 * each * LANES)
    cfg = (
        each,
        split,
        groups,
        group_clusters,
        rows.shape[0] // groups,
        own_groups,
        per_piece,
        feats,
    )
    smem = pl.BlockSpec(memory_space=pltpu.SMEM)
    vmem = pl.BlockSpec(memory_space=pltpu.VMEM)
    dests = own_groups * group_clusters // per_piece
    return pl.pallas_call(
        functools.partial(near_kernel, cfg),
        out_shape=pltpu.VMEM((dests, 2 * FS, per_piece // split * LANES), F32),
        in_specs=[smem] * 4 + [vmem] * 3,
        out_specs=vmem,
        scratch_shapes=[
            pltpu.VMEM((own_groups * group_clusters + 1, 2 * each, 8, LANES), F32),
            pltpu.VMEM((clusters, TERMS, CLUSTER), BF16),
            pltpu.VMEM((clusters, TERMS, 2 * LANES), BF16),
            pltpu.VMEM((clusters, feats, CLUSTER), BF16),
            pltpu.VMEM((CLUSTER, (2 + 2 * each) * LANES), F32),
            pltpu.VMEM((CLUSTER, (2 + 2 * each) * LANES), F32),
        ],
        compiler_params=pltpu.CompilerParams(vmem_limit_bytes=56 * 2**20),
        name="near_field",
    )(outside(coef), outside(rows), outside(cols), outside(live), held(geometry), held(values), held(jnp.asarray(sel)))


def per_device(history, points, areas, ownership, block_rows, block_cols, block_live):
    steps_local, elem_local = history.shape
    tm_count = lax.axis_size("tm")
    groups = lax.axis_size("elem")
    steps = steps_local * tm_count
    freqs = FS * tm_count
    width = elem_local // tm_count
    split = groups if groups == 2 and width % (2 * LANES) == 0 else 1
    each = FS // split
    shared = split == groups
    axes = ("tm", "elem") if shared else "tm"
    forward, inverse = packed_tables(steps, freqs, split)
    lap = laplace_table(freqs, steps).reshape(-1, each)
    coefs = np.concatenate([-lap.real / LOG_HALF, lap.imag / (2.0 * np.pi)], axis=1)
    coef = jnp.asarray(coefs.astype(np.float32).reshape(-1))

    own = ownership.reshape(1, elem_local)
    pieces = order_history(own, history, width)
    by_time = lax.all_to_all(
        pieces.reshape(tm_count * steps_local, width), "tm", split_axis=0, concat_axis=0, tiled=True
    )
    geometry = order_geometry(own, points, areas.reshape(1, elem_local))
    geometry = lax.all_gather(geometry, "elem", axis=0, tiled=True)
    spectra = forward_transform(jnp.asarray(forward), by_time, split)
    slab = lax.all_to_all(spectra, axes, split_axis=0, concat_axis=0, tiled=True)
    if not shared:
        slab = lax.all_gather(slab, "elem", axis=0, tiled=True)
    slab = slab.reshape(-1, 2 * FS, width // split)
    near = near_field(
        coef,
        block_rows,
        block_cols,
        block_live,
        geometry,
        slab,
        split,
        groups,
        groups if shared else 1,
    )
    near = lax.all_to_all(
        near.reshape(-1, width // split), axes, split_axis=0, concat_axis=0, tiled=True
    )
    rows = inverse_transform(jnp.asarray(inverse), near, split, tm_count)
    rows = lax.all_to_all(
        rows.reshape(steps, width), "tm", split_axis=0, concat_axis=0, tiled=True
    )
    return return_to_elements(own, rows.reshape(tm_count, steps_local, width))


def solution(mesh):
    return jax.shard_map(
        per_device,
        mesh=mesh,
        in_specs=(P("tm", "elem"), P(None, "elem"), P("elem"), P("elem"), P(), P(), P()),
        out_specs=P("tm", "elem"),
        check_vma=False,
    )
```

```python
import functools
import math

import jax
import jax.numpy as jnp
import numpy as np
from jax import lax
from jax.experimental import pallas as pl
from jax.experimental.pallas import tpu as pltpu
from jax.sharding import PartitionSpec as P

FS = 4
CLUSTER = 128
LANES = 128
LOG_HALF = 0.6931471805599453
SOFTEN = 0.05
INV_STEP = 4.0
FOUR_PI = 4.0 * math.pi
LOW = 256
GRID = 64
TERMS = 48
UNROLL = 32
RETURN_CHUNK = 4096
F32 = jnp.float32
BF16 = jnp.bfloat16


def fit(func, high, degree):
    nodes = (np.cos((np.arange(600) + 0.5) / 600 * np.pi) + 1) * (high / 2)
    series = np.polynomial.chebyshev.Chebyshev.fit(
        nodes, func(nodes), degree, domain=[0, high]
    )
    return [float(v) for v in series.convert(kind=np.polynomial.Polynomial).coef]


SIN_QUARTER = fit(lambda u: np.sin(np.pi / 2 * np.sqrt(u)) / np.sqrt(u), 0.25, 2)
COS_QUARTER = fit(lambda u: np.cos(np.pi / 2 * np.sqrt(u)), 0.25, 3)
HALF_SIN = 2.0 * SIN_QUARTER[-1] * COS_QUARTER[-1]
HALF_COS = 2.0 * SIN_QUARTER[-1] ** 2
ARCTAN = fit(lambda u: np.arctan(np.sqrt(u)) / np.sqrt(u) / (2 * np.pi), 1.0, 9)


def poly(coefs, u):
    total = jnp.full_like(u, coefs[-1])
    for value in coefs[-2::-1]:
        total = total * u + value
    return total


def monic(coefs, u):
    total = u + coefs[-2] / coefs[-1]
    for value in coefs[-3::-1]:
        total = total * u + value / coefs[-1]
    return total


def transform_tables(steps, freqs):
    time_ids = np.arange(steps)
    levels = np.arange(freqs)
    phase = (levels[:, None] * time_ids[None, :] % steps) * (2.0 * np.pi / steps)
    decay = np.exp2(-time_ids / steps)
    forward = np.stack([np.cos(phase) * decay, -np.sin(phase) * decay])
    weight = np.where(levels == 0, 1.0, 2.0)[:, None] / (decay * steps)[None, :]
    inverse = np.stack([np.cos(phase) * weight, -np.sin(phase) * weight])
    return forward, inverse


def laplace_table(freqs, steps):
    angles = np.arange(freqs) * (2.0 * np.pi / steps)
    zeta = math.exp(-LOG_HALF / steps) * np.exp(1j * angles)
    delta = (1.0 - zeta) + 0.5 * (1.0 - zeta) ** 2
    return INV_STEP * delta


def packed_tables(steps, freqs, split):
    forward, inverse = transform_tables(steps, freqs)
    each = FS // split
    dests = freqs // each
    fwd = np.zeros((dests, 2, split, each, split, steps), np.float64)
    inv = np.zeros((dests, 2, split, each, split, steps), np.float64)
    for half in range(split):
        rows = forward.reshape(2, dests, each, steps).transpose(1, 0, 2, 3)
        fwd[:, :, half, :, half, :] = rows
        rows = inverse.reshape(2, dests, each, steps).transpose(1, 0, 2, 3)
        inv[:, :, half, :, half, :] = rows
    fwd = fwd.reshape(dests * 2 * FS, split * steps)
    inv = inv.reshape(dests * 2 * FS, split * steps).T
    return fwd.astype(np.float32), np.ascontiguousarray(inv).astype(np.float32)


def held(x):
    return pltpu.with_memory_space_constraint(x, pltpu.VMEM)


def outside(x):
    return pltpu.with_memory_space_constraint(x, pltpu.HBM)


def parts_of(x, count):
    out = []
    for _ in range(count - 1):
        head = x.astype(BF16).astype(F32)
        out.append(head)
        x = x - head
    return out + [x]


def one_hot_low(low_row):
    width = low_row.shape[1]
    ids = lax.broadcasted_iota(jnp.int32, (LOW, width), 0)
    return jnp.where(ids == low_row, 1.0, 0.0).astype(BF16)


def stack_parts(read, count, rows, high_count, lhs_ref):
    group = 16 // rows
    for h in range(0, high_count, group):
        pieces = [parts_of(read(h + i), count) for i in range(group)]
        for part in range(count):
            block = jnp.concatenate([piece[part] for piece in pieces], axis=0)
            lhs_ref[h * rows : h * rows + 16, part * LOW : part * LOW + LOW] = block.astype(BF16)


def gather_body(own_ref, lhs_ref, rows, chunk, emit):
    count = lhs_ref.shape[1] // LOW
    each = 8 // rows
    stride = 16 if each == 1 else 8

    def step(c, _):
        at = pl.multiple_of(c * chunk, chunk)
        own = own_ref[:, pl.ds(at, chunk)]
        high = jnp.broadcast_to(own >> 8, (8, chunk))
        if each > 1:
            high = high - lax.broadcasted_iota(jnp.int32, (8, chunk), 0) // rows
        hot = one_hot_low(own & (LOW - 1))
        picked = jnp.dot(
            lhs_ref[...], jnp.concatenate([hot] * count, axis=0), preferred_element_type=F32
        )
        total = jnp.zeros((8, chunk), F32)
        for v in range(picked.shape[0] // stride):
            value = picked[stride * v : stride * v + 8]
            if stride == 16:
                value = value + picked[16 * v + 8 : 16 * v + 16]
            total += jnp.where(high == v * each, value, 0.0)
        emit(c, total)
        return 0

    lax.fori_loop(0, own_ref.shape[1] // chunk, step, 0, unroll=UNROLL)


def order_history_kernel(own_ref, hist_ref, out_ref, lhs_ref):
    elems = own_ref.shape[1]
    width = out_ref.shape[2]
    chunk = min(256, width)
    for h in range(elems // LOW):
        pieces = parts_of(hist_ref[:, LOW * h : LOW * h + LOW], 2)
        lhs_ref[16 * h : 16 * h + 16, :] = jnp.concatenate(pieces, axis=0).astype(BF16)
    per = width // chunk

    def emit(c, total):
        at = pl.multiple_of(lax.rem(c, per) * chunk, chunk)
        out_ref[c // per, :, pl.ds(at, chunk)] = total

    gather_body(own_ref, lhs_ref, 8, chunk, emit)


def order_history(own, history, width):
    steps, elems = history.shape
    return pl.pallas_call(
        order_history_kernel,
        out_shape=pltpu.VMEM((elems // width, steps, width), F32),
        scratch_shapes=[pltpu.VMEM((elems // LOW * 16, LOW), BF16)],
        name="order_history",
    )(outside(own), outside(history))


def order_geometry_kernel(own_ref, pts_ref, area_ref, out_ref, lhs_ref):
    elems = own_ref.shape[1]

    def read(h):
        at = slice(LOW * h, LOW * h + LOW)
        return jnp.concatenate([pts_ref[:, at], area_ref[:, at] * (1.0 / FOUR_PI)], axis=0)

    stack_parts(read, 3, 4, elems // LOW, lhs_ref)

    def emit(c, total):
        total = total + pltpu.roll(total, 4, 0)
        out_ref[2 * c] = total[:, :CLUSTER]
        out_ref[2 * c + 1] = total[:, CLUSTER:]

    gather_body(own_ref, lhs_ref, 4, 2 * CLUSTER, emit)


def order_geometry(own, points, areas):
    elems = own.shape[1]
    return pl.pallas_call(
        order_geometry_kernel,
        out_shape=jax.ShapeDtypeStruct((elems // CLUSTER, 8, CLUSTER), F32),
        scratch_shapes=[pltpu.VMEM((elems // LOW * 4, 3 * LOW), BF16)],
        name="order_geometry",
    )(outside(own), outside(points), outside(areas))


def return_kernel(own_ref, near_ref, out_ref, lhs_a, lhs_b, hot_a, hot_b, acc_ref):
    width = near_ref.shape[2]
    elems = own_ref.shape[1]
    high_count = elems // LOW
    chunk = lhs_a.shape[1]
    per = chunk // width
    acc_ref[...] = jnp.zeros_like(acc_ref)

    def scattered(c, lhs_ref, hot_ref):
        at = pl.multiple_of(c * chunk, chunk)
        own = own_ref[:, pl.ds(at, chunk)]
        hot_ref[...] = one_hot_low(own & (LOW - 1))
        high = jnp.broadcast_to(own >> 8, (8, chunk))
        for p in range(per):
            lanes = slice(p * width, p * width + width)
            pieces = parts_of(near_ref[c * per + p], 2)
            here = high[:, lanes]
            for h in range(high_count):
                mask = here == h
                both = [jnp.where(mask, piece, 0.0) for piece in pieces]
                lhs_ref[16 * h : 16 * h + 16, lanes] = jnp.concatenate(both, axis=0).astype(BF16)
        return lax.dot_general(
            lhs_ref[...], hot_ref[...], (((1,), (1,)), ((), ())), preferred_element_type=F32
        )

    def step(i, _):
        one = scattered(2 * i, lhs_a, hot_a)
        acc_ref[...] += one + scattered(2 * i + 1, lhs_b, hot_b)
        return 0

    lax.fori_loop(0, elems // (2 * chunk), step, 0)
    for h in range(high_count):
        out_ref[:, LOW * h : LOW * h + LOW] = (
            acc_ref[16 * h : 16 * h + 8, :] + acc_ref[16 * h + 8 : 16 * h + 16, :]
        )


def return_to_elements(own, values):
    pieces, steps, width = values.shape
    elems = own.shape[1]
    chunk = max(RETURN_CHUNK, width)
    return pl.pallas_call(
        return_kernel,
        out_shape=jax.ShapeDtypeStruct((steps, elems), F32),
        scratch_shapes=[pltpu.VMEM((elems // LOW * 16, chunk), BF16)] * 2
        + [pltpu.VMEM((LOW, chunk), BF16)] * 2
        + [pltpu.VMEM((elems // LOW * 16, LOW), F32)],
        name="return_to_elements",
    )(held(own), held(values))


def forward_kernel(split, table_ref, x_ref, out_ref):
    steps, width = x_ref.shape
    half = width // split
    stacked = jnp.concatenate([x_ref[:, half * s : half * s + half] for s in range(split)], axis=0)
    out_ref[...] = jnp.dot(
        table_ref[...], stacked, precision=lax.Precision.HIGHEST, preferred_element_type=F32
    )


def forward_transform(table, x, split):
    return pl.pallas_call(
        functools.partial(forward_kernel, split),
        out_shape=pltpu.VMEM((table.shape[0], x.shape[1] // split), F32),
        name="forward_transform",
    )(held(table), held(x))


def inverse_kernel(split, table_ref, x_ref, out_ref):
    total, half = x_ref.shape
    dests, steps_local, _ = out_ref.shape
    steps = dests * steps_local
    values = jnp.dot(
        table_ref[...], x_ref[...], precision=lax.Precision.HIGHEST, preferred_element_type=F32
    )
    for s in range(split):
        for d in range(dests):
            at = s * steps + d * steps_local
            out_ref[d, :, half * s : half * s + half] = values[at : at + steps_local]


def inverse_transform(table, x, split, dests):
    steps = table.shape[0] // split
    return pl.pallas_call(
        functools.partial(inverse_kernel, split),
        out_shape=pltpu.VMEM((dests, steps // dests, x.shape[1] * split), F32),
        name="inverse_transform",
    )(held(table), held(x))


def distance_terms(x):
    row = lax.broadcasted_iota(jnp.int32, x.shape, 0)
    first = row < 4
    third, seventh = row == 3, row == 7
    either = jnp.logical_or(third, seventh)
    zero, one = jnp.zeros_like(x), jnp.ones_like(x)

    def over_coords(v):
        v = jnp.where(either, 0.0, v)
        return v + pltpu.roll(v, 1, 0) + pltpu.roll(v, 2, 0) + pltpu.roll(v, 3, 0)

    def rows(top, bottom, three, seven):
        value = top if top is bottom else jnp.where(first, top, bottom)
        if three is seven:
            return jnp.where(either, three, value)
        return jnp.where(third, three, jnp.where(seventh, seven, value))

    def joined(*blocks):
        return jnp.concatenate([*blocks, zero], axis=0).astype(BF16)

    n = jnp.round(x * GRID)
    h = n * (1.0 / GRID)
    low = x - h
    l1, l2, l3 = parts_of(low, 3)
    n1, n2, n3 = parts_of(over_coords(n * n), 3)
    bias = over_coords((2.0 * h + low) * low)
    b1, b2, b3 = parts_of(bias, 3)
    left = joined(
        rows(n, n, n1, n2),
        rows(n, l1, n3, one),
        rows(l1, l1, one, one),
        rows(l2, l2, b1, b2),
        rows(l3, zero, b3, zero),
    )
    unit = 1.0 / GRID**2
    flat = one * unit
    exact = joined(
        rows(n * (-2.0 * unit), zero, flat, flat),
        rows(zero, zero, flat, n1 * unit),
        rows(zero, zero, n2 * unit, n3 * unit),
        zero,
        zero,
    )
    b1, b2, b3 = parts_of(bias + SOFTEN * SOFTEN, 3)
    g1, g2, g3 = (p * (-2.0 / GRID) for p in (l1, l2, l3))
    d1, d2, dh = (p * -2.0 for p in (l1, l2, h))
    rest = joined(
        rows(g1, g2, zero, zero),
        rows(g3, dh, zero, b1),
        rows(d1, d2, b2, b3),
        rows(dh, d1, one, one),
        rows(dh, zero, one, zero),
    )
    return left, exact, rest


def near_kernel(
    cfg,
    coef,
    rows,
    cols,
    live,
    geo_ref,
    val_ref,
    sel_ref,
    out_ref,
    acc_ref,
    col_ref,
    row_ref,
    feat_ref,
    buf_a,
    buf_b,
):
    each, split, groups, group_clusters, cap, own_groups, per_piece, feats = cfg
    my_group = lax.axis_index("elem")
    mine = lax.axis_index("tm")
    if own_groups == groups:
        mine = mine * split + my_group
    clusters = geo_ref.shape[0]
    per_half = per_piece // split
    pieces = group_clusters // per_piece
    acc_ref[...] = jnp.zeros_like(acc_ref)

    is_size = lax.broadcasted_iota(jnp.int32, (2 * FS, LANES), 0) >= FS

    def prepare(piece, _):
        for g in range(groups):
            index = piece * groups + g if own_groups == groups else g * pieces + piece
            chunk = val_ref[index]
            re, im = chunk[0:FS], chunk[FS : 2 * FS]
            ax, ay = jnp.abs(re), jnp.abs(im)
            large, small = jnp.maximum(ax, ay), jnp.minimum(ax, ay)
            q = small / jnp.maximum(large, 1e-37)
            turn = q * poly(ARCTAN, q * q)
            turn = jnp.where(ay > ax, 0.25 - turn, turn)
            turn = jnp.where(re < 0, 0.5 - turn, turn)
            turn = jnp.where(im < 0, -turn, turn)
            size = large * jnp.sqrt(1.0 + q * q)
            both = jnp.concatenate([turn, size], axis=0)
            for w in range(per_piece):
                c = g * group_clusters + piece * per_piece + w
                half, lane = w // per_half, (w % per_half) * LANES
                place = geo_ref[c]
                scale = jnp.where(is_size, place[3:4], 1.0)
                feature = both[:, lane : lane + LANES] * scale
                if half:
                    feature = pltpu.roll(feature, 2 * FS - half * each, 0)
                feat_ref[c] = jnp.concatenate(
                    [*parts_of(feature, 3), jnp.zeros_like(feature)], axis=0
                ).astype(BF16)
                left, exact, rest = distance_terms(place)
                col_ref[c] = left
                row_ref[c, :, :LANES] = exact
                row_ref[c, :, LANES:] = rest
        return 0

    lax.fori_loop(0, pieces, prepare, 0)

    decay = [coef[mine * 2 * each + f] for f in range(each)]
    turns = [coef[mine * 2 * each + each + f] for f in range(each)]
    sel = sel_ref[...].astype(BF16)
    lives = [live[g if own_groups == groups else my_group] for g in range(own_groups)]
    total_live = sum(lives)
    idle = own_groups * group_clusters

    def locate(b):
        slot, inside = jnp.int32(0), b
        for g in range(1, own_groups):
            over = inside >= lives[g - 1]
            moved = jnp.logical_and(over, slot == g - 1)
            inside = jnp.where(moved, inside - lives[g - 1], inside)
            slot = jnp.where(moved, g, slot)
        valid = b < total_live
        slot = jnp.where(valid, slot, 0)
        inside = jnp.where(valid, inside, 0)
        group = slot if own_groups == groups else my_group
        at = group * cap + inside
        row = rows[at]
        target = jnp.where(valid, slot * group_clusters + row, idle)
        return group * group_clusters + row, cols[at], target

    def load(b, buf):
        row, col, _ = locate(b)
        product = lambda a, b: lax.dot_general(
            a, b, (((0,), (0,)), ((), ())), preferred_element_type=F32
        )
        buf[:, : 2 * LANES] = product(col_ref[col], row_ref[row])
        buf[:, 2 * LANES :] = product(feat_ref[col], sel)

    def work(b, buf):
        _, _, target = locate(b)
        sums = [jnp.zeros((8, LANES), F32) for _ in range(3 * each)]
        for j in range(CLUSTER // 8):
            lane = lambda k: buf[8 * j : 8 * j + 8, LANES * k : LANES * k + LANES]
            square = lane(0) + lane(1)
            inv = lax.rsqrt(square)
            dist = square * inv
            for f in range(each):
                weight = jnp.exp2(decay[f] * dist) * (inv * lane(2 + each + f))
                t = lane(2 + f) - turns[f] * dist
                t = t - jnp.round(t)
                u = t * t
                s = t * monic(SIN_QUARTER, u)
                half_sin = s * monic(COS_QUARTER, u)
                half_cos = 1.0 / HALF_COS - s * s
                ws = weight * half_sin
                sums[3 * f] += weight
                sums[3 * f + 1] += ws * half_sin
                sums[3 * f + 2] += ws * half_cos
        for f in range(each):
            whole, squared, mixed = sums[3 * f : 3 * f + 3]
            acc_ref[target, f] += whole - (2.0 * HALF_SIN**2) * squared
            acc_ref[target, each + f] += (2.0 * HALF_SIN * HALF_COS) * mixed

    load(jnp.int32(0), buf_a)
    load(jnp.int32(1), buf_b)

    def pair(i, _):
        for q in range(0, 6, 2):
            work(6 * i + q, buf_a)
            load(6 * i + q + 2, buf_a)
            work(6 * i + q + 1, buf_b)
            load(6 * i + q + 3, buf_b)
        return 0

    lax.fori_loop(0, (total_live + 5) // 6, pair, 0)

    def finish(piece, _):
        for slot in range(own_groups):
            for w in range(per_piece):
                c = slot * group_clusters + piece * per_piece + w
                half, lane = w // per_half, (w % per_half) * LANES
                total = jnp.sum(acc_ref[c], axis=1)
                dest = piece * own_groups + slot
                for part in range(2):
                    first = part * FS + half * each
                    out_ref[dest, first : first + each, lane : lane + LANES] = total[
                        part * each : part * each + each
                    ]
        return 0

    lax.fori_loop(0, pieces, finish, 0)


def near_field(coef, rows, cols, live, geometry, values, split, groups, own_groups):
    each = FS // split
    clusters = geometry.shape[0]
    group_clusters = clusters // groups
    per_piece = values.shape[2] // LANES * split
    feats = 8 * FS
    sel = np.zeros((feats, 2 * each, LANES), np.float32)
    for part in range(3):
        for f in range(each):
            sel[part * 2 * FS + f, f] = 1.0
            sel[part * 2 * FS + FS + f, each + f] = 1.0
    sel = sel.reshape(feats, 2 * each * LANES)
    cfg = (
        each,
        split,
        groups,
        group_clusters,
        rows.shape[0] // groups,
        own_groups,
        per_piece,
        feats,
    )
    smem = pl.BlockSpec(memory_space=pltpu.SMEM)
    vmem = pl.BlockSpec(memory_space=pltpu.VMEM)
    dests = own_groups * group_clusters // per_piece
    return pl.pallas_call(
        functools.partial(near_kernel, cfg),
        out_shape=pltpu.VMEM((dests, 2 * FS, per_piece // split * LANES), F32),
        in_specs=[smem] * 4 + [vmem] * 3,
        out_specs=vmem,
        scratch_shapes=[
            pltpu.VMEM((own_groups * group_clusters + 1, 2 * each, 8, LANES), F32),
            pltpu.VMEM((clusters, TERMS, CLUSTER), BF16),
            pltpu.VMEM((clusters, TERMS, 2 * LANES), BF16),
            pltpu.VMEM((clusters, feats, CLUSTER), BF16),
            pltpu.VMEM((CLUSTER, (2 + 2 * each) * LANES), F32),
            pltpu.VMEM((CLUSTER, (2 + 2 * each) * LANES), F32),
        ],
        compiler_params=pltpu.CompilerParams(vmem_limit_bytes=56 * 2**20),
        name="near_field",
    )(outside(coef), outside(rows), outside(cols), outside(live), held(geometry), held(values), held(jnp.asarray(sel)))


def per_device(history, points, areas, ownership, block_rows, block_cols, block_live):
    steps_local, elem_local = history.shape
    tm_count = lax.axis_size("tm")
    groups = lax.axis_size("elem")
    steps = steps_local * tm_count
    freqs = FS * tm_count
    width = elem_local // tm_count
    split = groups if groups == 2 and width % (2 * LANES) == 0 else 1
    each = FS // split
    shared = split == groups
    axes = ("tm", "elem") if shared else "tm"
    forward, inverse = packed_tables(steps, freqs, split)
    lap = laplace_table(freqs, steps).reshape(-1, each)
    coefs = np.concatenate([-lap.real / LOG_HALF, lap.imag / (2.0 * np.pi)], axis=1)
    coef = jnp.asarray(coefs.astype(np.float32).reshape(-1))

    own = ownership.reshape(1, elem_local)
    pieces = order_history(own, history, width)
    by_time = lax.all_to_all(
        pieces.reshape(tm_count * steps_local, width), "tm", split_axis=0, concat_axis=0, tiled=True
    )
    geometry = order_geometry(own, points, areas.reshape(1, elem_local))
    geometry = lax.all_gather(geometry, "elem", axis=0, tiled=True)
    spectra = forward_transform(jnp.asarray(forward), by_time, split)
    slab = lax.all_to_all(spectra, axes, split_axis=0, concat_axis=0, tiled=True)
    if not shared:
        slab = lax.all_gather(slab, "elem", axis=0, tiled=True)
    slab = slab.reshape(-1, 2 * FS, width // split)
    near = near_field(
        coef,
        block_rows,
        block_cols,
        block_live,
        geometry,
        slab,
        split,
        groups,
        groups if shared else 1,
    )
    near = lax.all_to_all(
        near.reshape(-1, width // split), axes, split_axis=0, concat_axis=0, tiled=True
    )
    rows = inverse_transform(jnp.asarray(inverse), near, split, tm_count)
    rows = lax.all_to_all(
        rows.reshape(steps, width), "tm", split_axis=0, concat_axis=0, tiled=True
    )
    return return_to_elements(own, rows.reshape(tm_count, steps_local, width))


def solution(mesh):
    return jax.shard_map(
        per_device,
        mesh=mesh,
        in_specs=(P("tm", "elem"), P(None, "elem"), P("elem"), P("elem"), P(), P(), P()),
        out_specs=P("tm", "elem"),
        check_vma=False,
    )
```
